32 devices in a mesh: row: 8 (over z, x), col: 4 (over y, core).
Axes of the slice: x: 2, y: 2, z: 4, core: 2. Of those that a mesh axis runs over, the one named last changes fastest.
Arguments:
- hamiltonian: bfloat16 [2, 2048, 2048], P(None, 'row', 'col'), may hold values from -0.25 to 0.25
- basis_metric: bfloat16 [2048, 2048], P('row', 'col'), may hold values from -0.25 to 0.25
- density: bfloat16 [2, 2048, 2048], P(None, 'row', 'col'), may hold values from -6 to 6
- hamiltonian_keep: int32 [16, 16], P('row', 'col'), may hold values from 0 to 1, as said below
- metric_keep: int32 [16, 16], P('row', 'col'), may hold values from 0 to 1, as said below
- density_keep: int32 [16, 16], P('row', 'col'), may hold values from 0 to 1, as said below
- gradient_keep: int32 [16, 16], P('row', 'col'), may hold values 0 or 1
Outputs:
- gradient: float32 [2, 2048, 2048], P(None, 'row', 'col')
The draws below stay inside these ranges and needn't reach their ends.
Inputs may be any that keep to these rules, and one draw needn't show every extreme that they name: `hamiltonian_keep`: each block row has at most 4 blocks in the pattern, and some rows have exactly 4. `metric_keep`: each block row has at most 4 blocks in the pattern, and some rows have exactly 4. `density_keep`: each block row keeps at most 7 blocks, and some rows keep exactly 7.
All inputs are finite; a program needn't handle non-finite values. No bound on the sum of `gradient_keep` on one device may be relied on, other than what follows from the above.
Results may differ from the reference program's by a relative error of at most 0.0029.
Values may be sent and summed in bfloat16 or wider, within the bound.
No kernel may reach another device: no remote copies, remote signals or barrier semaphores. Data moves between devices by JAX's collectives and lax.ppermute only.
A program may use at most 64 MiB of HBM per device.

```python
import jax
import jax.numpy as jnp
from jax import lax

BLOCK = 128
NBLK = 16
N = 2048


def pattern(key, reach, extra):
    rows = jnp.arange(NBLK, dtype=jnp.int32)[:, None]
    cols = jnp.arange(NBLK, dtype=jnp.int32)[None, :]
    band = jnp.abs(rows - cols) <= reach
    scores = jax.random.randint(key, (NBLK, NBLK), 0, NBLK, dtype=jnp.int32) * NBLK + cols
    scores = jnp.where(band, -1, scores)
    tops, _ = lax.top_k(scores, extra)
    chosen = scores >= tops[:, extra - 1:extra]
    return jnp.where(band | chosen, 1, 0).astype(jnp.int32)


def draw_hamiltonian_keep(key, part):
    return pattern(jax.random.fold_in(key, 11), 1, 1)


def draw_metric_keep(key, part):
    return pattern(jax.random.fold_in(key, 23), 1, 1)


def draw_density_keep(key, part):
    return pattern(jax.random.fold_in(key, 37), 2, 2)


def touch_ends(drawn, own_key, low, high):
    longest = drawn.shape.index(max(drawn.shape))
    spots = []
    for shift in (0, 1):
        where = [jax.random.randint(jax.random.fold_in(own_key, axis), (), 0, length) for axis, length in enumerate(drawn.shape)]
        where[longest] = (where[longest] + shift) % drawn.shape[longest]
        spots.append(tuple(where))
    return drawn.at[spots[0]].set(low).at[spots[1]].set(high)


def steps_of(own_key, shape, split, least, largest):
    level, own = 1.0, jax.random.fold_in(own_key, 6)
    for dim, blocks in split:
        steps = jnp.exp(jax.random.uniform(jax.random.fold_in(own, dim), (blocks,), jnp.float32, least / len(split), largest / len(split)))
        level = level * jnp.repeat(steps, shape[dim] // blocks).reshape([-1 if axis == dim else 1 for axis in range(len(shape))])
    return level


def scatter_about(rng, shape, scale, most, pieces=(), kind=jnp.bfloat16):
    gain = steps_of(rng, shape, pieces, -0.22, 0.18) if pieces else 1.0
    values = jax.random.normal(rng, shape, jnp.float32) * scale * gain
    return jnp.minimum(jnp.maximum(values, -most), most).astype(kind)


def setup_inputs(seed: int = 0) -> dict:
    streams_of = jax.random.split(jax.random.key(seed), 8)
    hamiltonian = scatter_about(streams_of[0], (2, N, N), (4 * BLOCK) ** -0.5, 0.25, ((1, 8), (2, 4)))
    basis_metric = scatter_about(streams_of[1], (N, N), (4 * BLOCK) ** -0.5, 0.25, ((0, 8), (1, 4)))
    density = scatter_about(streams_of[2], (2, N, N), 1.0, 6.0, ((1, 8), (2, 4)))
    hamiltonian_keep = draw_hamiltonian_keep(jax.random.fold_in(streams_of[7], 71), 0)
    metric_keep = draw_metric_keep(jax.random.fold_in(streams_of[7], 71), 0)
    density_keep = draw_density_keep(jax.random.fold_in(streams_of[7], 71), 0)
    gradient_keep = touch_ends((jax.random.randint(streams_of[6], (NBLK, NBLK), 0, 4) < 3).astype(jnp.int32), jax.random.fold_in(streams_of[6], 1), 0, 1)
    return {"hamiltonian": hamiltonian, "basis_metric": basis_metric, "density": density, "hamiltonian_keep": hamiltonian_keep, "metric_keep": metric_keep, "density_keep": density_keep, "gradient_keep": gradient_keep}


def widen(keep):
    return jnp.repeat(jnp.repeat(keep, BLOCK, axis=0), BLOCK, axis=1) > 0


def matmul(left, right):
    return jnp.dot(left.astype(jnp.float32), right.astype(jnp.float32), precision=lax.Precision.HIGHEST)


def reference(hamiltonian, basis_metric, density, hamiltonian_keep, metric_keep, density_keep, gradient_keep):
    kohn_sham = jnp.where(widen(hamiltonian_keep)[None], hamiltonian, jnp.zeros_like(hamiltonian))
    smat = jnp.where(widen(metric_keep), basis_metric, jnp.zeros_like(basis_metric))
    filtered = jnp.where(widen(density_keep)[None], density, jnp.zeros_like(density))
    grad_mask = widen(gradient_keep)
    results = []
    for spin_index in range(2):
        hprod = matmul(kohn_sham[spin_index], filtered[spin_index]).astype(jnp.bfloat16)
        sprod = matmul(smat, filtered[spin_index]).astype(jnp.bfloat16)
        commut = matmul(hprod, smat) - matmul(sprod, kohn_sham[spin_index])
        results.append(jnp.where(grad_mask, commut, jnp.zeros_like(commut)))
    return jnp.stack(results, axis=0)
```

```python
import functools

import jax
import jax.numpy as jnp
from jax import lax
from jax.experimental import pallas as pl
from jax.experimental.pallas import tpu as pltpu
from jax.sharding import PartitionSpec as P

BLOCK = 128
OPERATOR_SLOTS = 4
DENSITY_SLOTS = 7

ANY = pl.BlockSpec(memory_space=pl.ANY)
VMEM = pl.BlockSpec(memory_space=pltpu.VMEM)
SMEM = pl.BlockSpec(memory_space=pltpu.SMEM)


def estimate(flops, nbytes):
    return pl.CostEstimate(flops=flops, bytes_accessed=nbytes, transcendentals=0)


def split_kernel(place, density, hamiltonian, metric, *rest):
    outs, sems = rest[:4], rest[4]
    spin, row = place[0], place[1]
    copies = []
    for v in (2, 3, 1, 0):
        other_spin = spin if v < 2 else 1 - spin
        other_row = row if v % 2 == 0 else 1 - row
        rows = pl.ds(pl.multiple_of(other_row * BLOCK, BLOCK), BLOCK)
        sources = (density.at[other_spin, rows], hamiltonian.at[other_spin, rows], metric.at[rows])
        for n, source in enumerate(sources):
            copies.append(pltpu.make_async_copy(source, outs[v].at[n], sems.at[v * 3 + n]))
    for copy in copies:
        copy.start()
    for copy in copies:
        copy.wait()


def pack_kernel(sources, col, keep, *refs):
    ins, dens_out, oper_out = refs[:sources], refs[sources], refs[sources + 1]
    per = ins[0].shape[2] // BLOCK
    dens_out[...] = jnp.zeros_like(dens_out)
    oper_out[...] = jnp.zeros_like(oper_out)
    here = col[0]
    for mat, (out, first) in enumerate(((dens_out, 0), (oper_out, 0), (oper_out, OPERATOR_SLOTS))):
        flags = [[keep[m, mat, b] for b in range(per)] for m in range(sources)]
        counts = [functools.reduce(lambda p, q: p + q, f) for f in flags]
        for m in range(sources):
            slot = jnp.int32(first)
            for n in range(sources):
                if n != m:
                    slot += jnp.where((here ^ n) < (here ^ m), counts[n], 0)
            for b in range(per):

                @pl.when(flags[m][b] > 0)
                def _(slot=slot, m=m, b=b):
                    out[slot] = ins[m][mat, :, b * BLOCK : (b + 1) * BLOCK]

                slot += flags[m][b]


def row_of(place, key, layers):
    shift, flip, other = key
    layer = place[0] - shift
    layer = jnp.where(layer < 0, layer + layers, layer)
    side = place[1] if flip == 0 else 1 - place[1]
    half = place[2] if other == 0 else 1 - place[2]
    return (layer * 2 + side) * 2 + half


def fetch(place, keys, layers, bufs, held, sems):
    copies = [
        pltpu.make_async_copy(buf, held.at[row_of(place, key, layers)], sems.at[n])
        for n, (key, buf) in enumerate(zip(keys, bufs, strict=True))
    ]
    for copy in copies:
        copy.start()
    return copies


def first_kernel(keys, layers, place, mine, cols, own, *refs):
    count = len(keys)
    bufs, out, held, acc, sems = refs[:count], *refs[count:]
    copies = fetch(place, keys, layers, bufs, held, sems)
    acc[...] = jnp.zeros_like(acc)
    for copy in copies:
        copy.wait()
    nblk = held.shape[0]
    for u in range(2 * OPERATOR_SLOTS):
        k = mine[u]
        left = own[u]
        base = (u // OPERATOR_SLOTS) * nblk
        for t in range(DENSITY_SLOTS):
            acc[base + cols[k, t]] += jnp.dot(left, held[k, t], preferred_element_type=jnp.float32)
    out[...] = acc[...].astype(out.dtype)


def second_kernel(keys, layers, place, cols, prods, *refs):
    count = len(keys)
    bufs, outs, (held, acc, sems) = refs[:count], refs[count : count + 4], refs[count + 4 :]
    copies = fetch(place, keys, layers, bufs, held, sems)
    acc[...] = jnp.zeros_like(acc)
    for copy in copies:
        copy.wait()
    nblk = held.shape[0]

    def step(k, carry):
        hp, sp = prods[k], prods[nblk + k]
        for t in range(OPERATOR_SLOTS):
            u = OPERATOR_SLOTS + t
            acc[cols[k, u]] += jnp.dot(hp, held[k, u], preferred_element_type=jnp.float32)
            acc[cols[k, t]] -= jnp.dot(sp, held[k, t], preferred_element_type=jnp.float32)
        return carry

    lax.fori_loop(0, nblk, step, 0)
    per = outs[0].shape[0]
    for v in range(4):
        for b in range(per):
            outs[v][b] = acc[place[3 + v] * per + b]


def join_kernel(place, keep, *refs):
    ins, out = refs[:4], refs[4]
    per = ins[0].shape[0]
    for v in range(4):
        spin = place[0] if v < 2 else 1 - place[0]
        row = place[1] if v % 2 == 0 else 1 - place[1]
        rows = pl.ds(pl.multiple_of(row * BLOCK, BLOCK), BLOCK)
        for b in range(per):
            value = ins[v][b]
            out[spin, rows, b * BLOCK : (b + 1) * BLOCK] = jnp.where(
                keep[row, b] > 0, value, jnp.zeros_like(value)
            )


def columns_of(keep, slots):
    n = keep.shape[1]
    index = jnp.arange(n, dtype=jnp.int32)
    before = (index[:, None] < index[None, :]).astype(jnp.int32)
    rank = jnp.sum(keep[:, :, None] * before[None], axis=1)
    hit = (rank[:, None, :] == jnp.arange(slots, dtype=jnp.int32)[None, :, None]) & (keep > 0)[:, None, :]
    return jnp.sum(jnp.where(hit, index[None, None, :], 0), axis=2)


def body(nrow, ncol, hamiltonian, metric, density, ham_keep, met_keep, dens_keep, grad_keep):
    layers, half = nrow // 2, ncol // 2
    per = ham_keep.shape[1]
    nblk = ham_keep.shape[0] * nrow
    width = per * BLOCK
    bf16, f32, i32 = jnp.bfloat16, jnp.float32, jnp.int32

    def by_row(pairs):
        return lambda a: lax.ppermute(a, "row", pairs)

    def by_mask(mask):
        return lambda a: lax.ppermute(a, "col", [(c, c ^ mask) for c in range(ncol)])

    def variant(mask):
        return (2 if mask >= half else 0) + (mask & 1)

    up = by_row([(r, (r + 2) % nrow) for r in range(nrow)])
    across = by_row([(r, r ^ 1) for r in range(nrow)])
    twin = by_mask(1)

    row, col = lax.axis_index("row").astype(i32), lax.axis_index("col").astype(i32)
    spin, part = col // half, col % 2
    z, x = row // 2, row % 2
    masks = (0, 1, half, half + 1)

    keeps = (jnp.stack([dens_keep, ham_keep, met_keep]) > 0).astype(i32)
    spread = lax.all_gather(keeps, ("row", "col"))

    split = pl.pallas_call(
        split_kernel,
        out_shape=[jax.ShapeDtypeStruct((3, BLOCK, width), bf16)] * 4,
        in_specs=[SMEM, ANY, ANY, ANY],
        out_specs=[ANY] * 4,
        scratch_shapes=[pltpu.SemaphoreType.DMA((12,))],
        cost_estimate=estimate(0, 24 * BLOCK * width * 2),
        name="split",
    )(jnp.stack([spin, part]), density, hamiltonian, metric)
    got = {m: by_mask(m)(split[variant(m)]) for m in reversed(range(1, ncol))}
    got[0] = split[0]
    keep_rows = [lax.dynamic_index_in_dim(keeps, part ^ d, 1, keepdims=False) for d in (0, 1)]
    keep_got = jnp.stack(
        [keep_rows[0]] + [by_mask(m)(keep_rows[m & 1]) for m in range(1, ncol)]
    )

    dens, oper = pl.pallas_call(
        functools.partial(pack_kernel, ncol),
        out_shape=[
            jax.ShapeDtypeStruct((DENSITY_SLOTS, BLOCK, BLOCK), bf16),
            jax.ShapeDtypeStruct((2 * OPERATOR_SLOTS, BLOCK, BLOCK), bf16),
        ],
        in_specs=[SMEM, SMEM] + [VMEM] * ncol,
        out_specs=[VMEM, VMEM],
        cost_estimate=estimate(0, ncol * 3 * BLOCK * width * 2),
        name="pack",
    )(col[None], keep_got, *[got[m] for m in range(ncol)])

    dens_bufs, oper_bufs = {}, {}
    curs = [dens, oper]
    for t in range(layers):
        nexts = []
        for bufs, cur in zip((dens_bufs, oper_bufs), curs, strict=True):
            side = across(cur)
            if t < layers - 1:
                new, side = lax.optimization_barrier((up(cur), side))
                nexts.append(new)
            bufs[t, 0, 0], bufs[t, 1, 0] = cur, side
            bufs[t, 0, 1], bufs[t, 1, 1] = twin(cur), twin(side)
        curs = nexts
    keys = list(dens_bufs)

    tables = spread.reshape(nrow, ncol, 3, 2, per).transpose(2, 0, 3, 1, 4).reshape(3, nblk, nblk)
    dens_cols = columns_of(tables[0], DENSITY_SLOTS)
    oper_cols = jnp.concatenate(
        [columns_of(tables[1], OPERATOR_SLOTS), columns_of(tables[2], OPERATOR_SLOTS)], axis=1
    )
    mine = lax.dynamic_index_in_dim(oper_cols, 2 * row + part, 0, keepdims=False)
    place = jnp.stack([z, x, part] + [col ^ m for m in masks])

    prods = pl.pallas_call(
        functools.partial(first_kernel, keys, layers),
        out_shape=jax.ShapeDtypeStruct((2 * nblk, BLOCK, BLOCK), bf16),
        in_specs=[SMEM, SMEM, SMEM, VMEM] + [ANY] * len(keys),
        out_specs=VMEM,
        scratch_shapes=[
            pltpu.VMEM((nblk, DENSITY_SLOTS, BLOCK, BLOCK), bf16),
            pltpu.VMEM((2 * nblk, BLOCK, BLOCK), f32),
            pltpu.SemaphoreType.DMA((len(keys),)),
        ],
        cost_estimate=estimate(56 * 2 * BLOCK**3, nblk * 9 * BLOCK * BLOCK * 2),
        name="first",
    )(place, mine, dens_cols, oper, *[dens_bufs[k] for k in keys])

    outs = pl.pallas_call(
        functools.partial(second_kernel, keys, layers),
        out_shape=[jax.ShapeDtypeStruct((per, BLOCK, BLOCK), f32)] * 4,
        in_specs=[SMEM, SMEM, VMEM] + [ANY] * len(keys),
        out_specs=[VMEM] * 4,
        scratch_shapes=[
            pltpu.VMEM((nblk, 2 * OPERATOR_SLOTS, BLOCK, BLOCK), bf16),
            pltpu.VMEM((nblk, BLOCK, BLOCK), f32),
            pltpu.SemaphoreType.DMA((len(keys),)),
        ],
        cost_estimate=estimate(nblk * 16 * BLOCK**3, nblk * 12 * BLOCK * BLOCK * 2),
        name="second",
    )(place, oper_cols, prods, *[oper_bufs[k] for k in keys])

    back = [outs[0]] + [by_mask(m)(o) for m, o in zip(masks[1:], outs[1:], strict=True)]
    return pl.pallas_call(
        join_kernel,
        out_shape=jax.ShapeDtypeStruct((2, 2 * BLOCK, width), f32),
        in_specs=[SMEM, SMEM] + [VMEM] * 4,
        out_specs=VMEM,
        cost_estimate=estimate(0, 8 * BLOCK * width * 4),
        name="join",
    )(jnp.stack([spin, part]), grad_keep, *back)


def solution(mesh):
    grid = P("row", "col")
    spins = P(None, "row", "col")
    return jax.shard_map(
        functools.partial(body, mesh.shape["row"], mesh.shape["col"]),
        mesh=mesh,
        in_specs=(spins, grid, spins, grid, grid, grid, grid),
        out_specs=spins,
        check_vma=False,
    )
```

```python
import functools

import jax
import jax.numpy as jnp
from jax import lax
from jax.experimental import pallas as pl
from jax.experimental.pallas import tpu as pltpu
from jax.sharding import PartitionSpec as P

BLOCK = 128
OPERATOR_SLOTS = 4
DENSITY_SLOTS = 7
TAIL = 16

ANY = pl.BlockSpec(memory_space=pl.ANY)
VMEM = pl.BlockSpec(memory_space=pltpu.VMEM)
SMEM = pl.BlockSpec(memory_space=pltpu.SMEM)


def estimate(flops, nbytes):
    return pl.CostEstimate(flops=flops, bytes_accessed=nbytes, transcendentals=0)


def split_kernel(place, density, hamiltonian, metric, *outs):
    spin, row = place[0], place[1]
    for v in (2, 3, 1, 0):
        other_spin = spin if v < 2 else 1 - spin
        other_row = row if v % 2 == 0 else 1 - row
        rows = pl.ds(pl.multiple_of(other_row * BLOCK, BLOCK), BLOCK)
        outs[v][0] = density[other_spin, rows, :]
        outs[v][1] = hamiltonian[other_spin, rows, :]
        outs[v][2] = metric[rows, :]


def slot_rows(slot):
    start = slot * BLOCK
    return pl.ds(start if isinstance(slot, int) else pl.multiple_of(start, BLOCK), BLOCK)


def pack_kernel(sources, col, keep, *refs):
    ins, dens_out, oper_out = refs[:sources], refs[sources], refs[sources + 1]
    per = ins[0].shape[2] // BLOCK
    here = col[0]
    lane = lax.broadcasted_iota(jnp.int32, (TAIL, BLOCK), 1)
    plans = (
        (dens_out, DENSITY_SLOTS, ((0, 0),)),
        (oper_out, 2 * OPERATOR_SLOTS, ((1, 0), (2, OPERATOR_SLOTS))),
    )
    for out, slots, mats in plans:
        out[...] = jnp.zeros_like(out)
        tail = jnp.zeros((TAIL, BLOCK), jnp.int32)
        for mat, first in mats:
            flags = [[keep[m, mat, b] for b in range(per)] for m in range(sources)]
            counts = [functools.reduce(lambda p, q: p + q, f) for f in flags]
            for m in range(sources):
                slot = jnp.int32(first)
                for n in range(sources):
                    if n != m:
                        slot += jnp.where((here ^ n) < (here ^ m), counts[n], 0)
                for b in range(per):

                    @pl.when(flags[m][b] > 0)
                    def _(slot=slot, mat=mat, m=m, b=b, out=out):
                        out[slot_rows(slot), :] = ins[m][mat, :, b * BLOCK : (b + 1) * BLOCK]

                    target = jnp.where(flags[m][b] > 0, slot, -1)
                    tail = jnp.where(lane == target, (here ^ m) * per + b, tail)
                    slot += flags[m][b]
        out[slots * BLOCK :, :] = tail.astype(jnp.float32).astype(out.dtype)


def row_of(place, key, layers):
    shift, flip, other = key
    layer = place[0] - shift
    layer = jnp.where(layer < 0, layer + layers, layer)
    side = place[1] if flip == 0 else 1 - place[1]
    half = place[2] if other == 0 else 1 - place[2]
    return (layer * 2 + side) * 2 + half


def fetch(place, keys, layers, bufs, held, sems):
    copies = [
        pltpu.make_async_copy(buf, held.at[row_of(place, key, layers)], sems.at[n])
        for n, (key, buf) in enumerate(zip(keys, bufs, strict=True))
    ]
    for copy in copies:
        copy.start()
    return copies


def tail_of(block):
    return block.astype(jnp.float32)[:1].astype(jnp.int32)


def first_kernel(keys, layers, place, own, *refs):
    count = len(keys)
    bufs, out, held, acc, tails, cols, sems = refs[:count], *refs[count:]
    nblk = held.shape[0]
    copies = fetch(place, keys, layers, bufs, held, sems)
    acc[...] = jnp.zeros_like(acc)
    tails[nblk : nblk + 1, :] = tail_of(own[2 * OPERATOR_SLOTS * BLOCK :, :])
    for copy in copies:
        copy.wait()
    for k in range(nblk):
        tails[k : k + 1, :] = tail_of(held[k, DENSITY_SLOTS * BLOCK :, :])
    pltpu.sync_copy(tails, cols)
    for u in range(2 * OPERATOR_SLOTS):
        k = cols[nblk, u]
        left = own[u * BLOCK : (u + 1) * BLOCK, :]
        base = (u // OPERATOR_SLOTS) * nblk
        for t in range(DENSITY_SLOTS):
            right = held[k, t * BLOCK : (t + 1) * BLOCK, :]
            acc[base + cols[k, t]] += jnp.dot(left, right, preferred_element_type=jnp.float32)
    out[...] = acc[...].astype(out.dtype)


def second_kernel(keys, layers, place, prods, *refs):
    count = len(keys)
    bufs, outs, (held, acc, tails, cols, sems) = refs[:count], refs[count : count + 4], refs[count + 4 :]
    nblk = held.shape[0]
    copies = fetch(place, keys, layers, bufs, held, sems)
    acc[...] = jnp.zeros_like(acc)
    for copy in copies:
        copy.wait()
    for k in range(nblk):
        tails[k : k + 1, :] = tail_of(held[k, 2 * OPERATOR_SLOTS * BLOCK :, :])
    pltpu.sync_copy(tails, cols)

    def step(k, carry):
        hp, sp = prods[k], prods[nblk + k]
        for t in range(OPERATOR_SLOTS):
            u = OPERATOR_SLOTS + t
            met = held[k, u * BLOCK : (u + 1) * BLOCK, :]
            ham = held[k, t * BLOCK : (t + 1) * BLOCK, :]
            acc[cols[k, u]] += jnp.dot(hp, met, preferred_element_type=jnp.float32)
            acc[cols[k, t]] -= jnp.dot(sp, ham, preferred_element_type=jnp.float32)
        return carry

    lax.fori_loop(0, nblk, step, 0)
    per = outs[0].shape[0]
    for v in range(4):
        for b in range(per):
            outs[v][b] = acc[place[3 + v] * per + b]


def join_kernel(place, keep, *refs):
    ins, out = refs[:4], refs[4]
    per = ins[0].shape[0]
    for v in range(4):
        spin = place[0] if v < 2 else 1 - place[0]
        row = place[1] if v % 2 == 0 else 1 - place[1]
        rows = pl.ds(pl.multiple_of(row * BLOCK, BLOCK), BLOCK)
        for b in range(per):
            value = ins[v][b]
            out[spin, rows, b * BLOCK : (b + 1) * BLOCK] = jnp.where(
                keep[row, b] > 0, value, jnp.zeros_like(value)
            )


def body(nrow, ncol, hamiltonian, metric, density, ham_keep, met_keep, dens_keep, grad_keep):
    layers, half = nrow // 2, ncol // 2
    per = ham_keep.shape[1]
    nblk = ham_keep.shape[0] * nrow
    width = per * BLOCK
    bf16, f32, i32 = jnp.bfloat16, jnp.float32, jnp.int32

    def by_row(pairs):
        return lambda a: lax.ppermute(a, "row", pairs)

    def by_mask(mask):
        return lambda a: lax.ppermute(a, "col", [(c, c ^ mask) for c in range(ncol)])

    def variant(mask):
        return (2 if mask >= half else 0) + (mask & 1)

    up = by_row([(r, (r + 2) % nrow) for r in range(nrow)])
    across = by_row([(r, r ^ 1) for r in range(nrow)])
    twin = by_mask(1)

    row, col = lax.axis_index("row").astype(i32), lax.axis_index("col").astype(i32)
    spin, part = col // half, col % 2
    z, x = row // 2, row % 2
    masks = (0, 1, half, half + 1)
    dens_rows, oper_rows = DENSITY_SLOTS * BLOCK + TAIL, 2 * OPERATOR_SLOTS * BLOCK + TAIL

    keeps = (jnp.stack([dens_keep, ham_keep, met_keep]) > 0).astype(i32)

    split = pl.pallas_call(
        split_kernel,
        out_shape=[jax.ShapeDtypeStruct((3, BLOCK, width), bf16)] * 4,
        in_specs=[SMEM, VMEM, VMEM, VMEM],
        out_specs=[VMEM] * 4,
        cost_estimate=estimate(0, 24 * BLOCK * width * 2),
        name="split",
    )(jnp.stack([spin, part]), density, hamiltonian, metric)
    got = {m: by_mask(m)(split[variant(m)]) for m in reversed(range(1, ncol))}
    got[0] = split[0]
    keep_rows = [lax.dynamic_index_in_dim(keeps, part ^ d, 1, keepdims=False) for d in (0, 1)]
    keep_got = jnp.stack(
        [keep_rows[0]] + [by_mask(m)(keep_rows[m & 1]) for m in range(1, ncol)]
    )

    dens, oper = pl.pallas_call(
        functools.partial(pack_kernel, ncol),
        out_shape=[
            jax.ShapeDtypeStruct((dens_rows, BLOCK), bf16),
            jax.ShapeDtypeStruct((oper_rows, BLOCK), bf16),
        ],
        in_specs=[SMEM, SMEM] + [VMEM] * ncol,
        out_specs=[VMEM, VMEM],
        cost_estimate=estimate(0, ncol * 3 * BLOCK * width * 2),
        name="pack",
    )(col[None], keep_got, *[got[m] for m in range(ncol)])

    dens_bufs, oper_bufs = {}, {}
    curs = [dens, oper]
    for t in range(layers):
        nexts = []
        for bufs, cur in zip((dens_bufs, oper_bufs), curs, strict=True):
            side = across(cur)
            if t < layers - 1:
                new, side = lax.optimization_barrier((up(cur), side))
                nexts.append(new)
            bufs[t, 0, 0], bufs[t, 1, 0] = cur, side
            bufs[t, 0, 1], bufs[t, 1, 1] = twin(cur), twin(side)
        curs = nexts
    keys = list(dens_bufs)

    place = jnp.stack([z, x, part] + [col ^ m for m in masks])

    prods = pl.pallas_call(
        functools.partial(first_kernel, keys, layers),
        out_shape=jax.ShapeDtypeStruct((2 * nblk, BLOCK, BLOCK), bf16),
        in_specs=[SMEM, VMEM] + [ANY] * len(keys),
        out_specs=VMEM,
        scratch_shapes=[
            pltpu.VMEM((nblk, dens_rows, BLOCK), bf16),
            pltpu.VMEM((2 * nblk, BLOCK, BLOCK), f32),
            pltpu.VMEM((nblk + 8, BLOCK), i32),
            pltpu.SMEM((nblk + 8, BLOCK), i32),
            pltpu.SemaphoreType.DMA((len(keys),)),
        ],
        cost_estimate=estimate(56 * 2 * BLOCK**3, nblk * 9 * BLOCK * BLOCK * 2),
        name="first",
    )(place, oper, *[dens_bufs[k] for k in keys])

    outs = pl.pallas_call(
        functools.partial(second_kernel, keys, layers),
        out_shape=[jax.ShapeDtypeStruct((per, BLOCK, BLOCK), f32)] * 4,
        in_specs=[SMEM, VMEM] + [ANY] * len(keys),
        out_specs=[VMEM] * 4,
        scratch_shapes=[
            pltpu.VMEM((nblk, oper_rows, BLOCK), bf16),
            pltpu.VMEM((nblk, BLOCK, BLOCK), f32),
            pltpu.VMEM((nblk, BLOCK), i32),
            pltpu.SMEM((nblk, BLOCK), i32),
            pltpu.SemaphoreType.DMA((len(keys),)),
        ],
        cost_estimate=estimate(nblk * 16 * BLOCK**3, nblk * 12 * BLOCK * BLOCK * 2),
        name="second",
    )(place, prods, *[oper_bufs[k] for k in keys])

    back = [outs[0]] + [by_mask(m)(o) for m, o in zip(masks[1:], outs[1:], strict=True)]
    return pl.pallas_call(
        join_kernel,
        out_shape=jax.ShapeDtypeStruct((2, 2 * BLOCK, width), f32),
        in_specs=[SMEM, SMEM] + [VMEM] * 4,
        out_specs=VMEM,
        cost_estimate=estimate(0, 8 * BLOCK * width * 4),
        name="join",
    )(jnp.stack([spin, part]), grad_keep, *back)


def solution(mesh):
    grid = P("row", "col")
    spins = P(None, "row", "col")
    return jax.shard_map(
        functools.partial(body, mesh.shape["row"], mesh.shape["col"]),
        mesh=mesh,
        in_specs=(spins, grid, spins, grid, grid, grid, grid),
        out_specs=spins,
        check_vma=False,
    )
```

```python
import functools

import jax
import jax.numpy as jnp
from jax import lax
from jax.experimental import pallas as pl
from jax.experimental.pallas import tpu as pltpu
from jax.sharding import PartitionSpec as P

BLOCK = 128
OPERATOR_SLOTS = 4
DENSITY_SLOTS = 7
TAIL = 16

ANY = pl.BlockSpec(memory_space=pl.ANY)
VMEM = pl.BlockSpec(memory_space=pltpu.VMEM)
SMEM = pl.BlockSpec(memory_space=pltpu.SMEM)


def estimate(flops, nbytes):
    return pl.CostEstimate(flops=flops, bytes_accessed=nbytes, transcendentals=0)


def split_kernel(place, density, hamiltonian, metric, *outs):
    spin, row = place[0], place[1]
    for v in (2, 3, 1, 0):
        other_spin = spin if v < 2 else 1 - spin
        other_row = row if v % 2 == 0 else 1 - row
        rows = pl.ds(pl.multiple_of(other_row * BLOCK, BLOCK), BLOCK)
        outs[v][...] = density[other_spin, rows, :]
        outs[4 + v][...] = hamiltonian[other_spin, rows, :]
        if v < 2:
            outs[8 + v][...] = metric[rows, :]


def slot_rows(slot):
    start = slot * BLOCK
    return pl.ds(start if isinstance(slot, int) else pl.multiple_of(start, BLOCK), BLOCK)


def pack_kernel(sources, mat, slots, col, keep, *refs):
    ins, out = refs[:sources], refs[sources]
    per = ins[0].shape[1] // BLOCK
    here = col[0]
    lane = lax.broadcasted_iota(jnp.int32, (TAIL, BLOCK), 1)
    out[...] = jnp.zeros_like(out)
    tail = jnp.zeros((TAIL, BLOCK), jnp.int32)
    flags = [[keep[m, mat, b] for b in range(per)] for m in range(sources)]
    counts = [functools.reduce(lambda p, q: p + q, f) for f in flags]
    for m in range(sources):
        slot = jnp.int32(0)
        for n in range(sources):
            if n != m:
                slot += jnp.where((here ^ n) < (here ^ m), counts[n], 0)
        for b in range(per):

            @pl.when(flags[m][b] > 0)
            def _(slot=slot, m=m, b=b):
                out[slot_rows(slot), :] = ins[m][:, b * BLOCK : (b + 1) * BLOCK]

            target = jnp.where(flags[m][b] > 0, slot, -1)
            tail = jnp.where(lane == target, (here ^ m) * per + b, tail)
            slot += flags[m][b]
    out[slots * BLOCK :, :] = tail.astype(jnp.float32).astype(out.dtype)


def row_of(place, key, layers):
    shift, flip, other = key
    layer = place[0] - shift
    layer = jnp.where(layer < 0, layer + layers, layer)
    side = place[1] if flip == 0 else 1 - place[1]
    half = place[2] if other == 0 else 1 - place[2]
    return (layer * 2 + side) * 2 + half


def fetch(place, keys, layers, bufs, held, sems):
    copies = [
        pltpu.make_async_copy(buf, held.at[row_of(place, key, layers)], sems.at[n])
        for n, (key, buf) in enumerate(zip(keys, bufs, strict=True))
    ]
    for copy in copies:
        copy.start()
    return copies


def tail_of(block):
    return block.astype(jnp.float32)[:1].astype(jnp.int32)


def read_tails(slots, held, tails):
    for k in range(held.shape[0]):
        tails[k : k + 1, :] = tail_of(held[k, slots * BLOCK :, :])


def first_kernel(keys, layers, place, ham, met, *refs):
    count = len(keys)
    bufs, out, held, acc, tails, cols, sems = refs[:count], *refs[count:]
    nblk = held.shape[0]
    copies = fetch(place, keys, layers, bufs, held, sems)
    acc[...] = jnp.zeros_like(acc)
    owns = (ham, met)
    for n, own in enumerate(owns):
        tails[nblk + n : nblk + n + 1, :] = tail_of(own[OPERATOR_SLOTS * BLOCK :, :])
    for copy in copies:
        copy.wait()
    read_tails(DENSITY_SLOTS, held, tails)
    pltpu.sync_copy(tails, cols)
    for n, own in enumerate(owns):
        for u in range(OPERATOR_SLOTS):
            k = cols[nblk + n, u]
            left = own[u * BLOCK : (u + 1) * BLOCK, :]
            for t in range(DENSITY_SLOTS):
                right = held[k, t * BLOCK : (t + 1) * BLOCK, :]
                acc[n * nblk + cols[k, t]] += jnp.dot(left, right, preferred_element_type=jnp.float32)
    out[...] = acc[...].astype(out.dtype)


def second_kernel(keys, layers, which, place, prods, *refs):
    count = len(keys)
    bufs, rest = refs[:count], refs[count:]
    if which == 0:
        acc, held, tails, cols, sems = rest
        outs = ()
    else:
        before, *outs, acc, held, tails, cols, sems = rest
    nblk = held.shape[0]
    copies = fetch(place, keys, layers, bufs, held, sems)
    if which == 0:
        acc[...] = jnp.zeros_like(acc)
    else:
        acc[...] = before[...]
    for copy in copies:
        copy.wait()
    read_tails(OPERATOR_SLOTS, held, tails)
    pltpu.sync_copy(tails, cols)

    def step(k, carry):
        left = prods[which * nblk + k]
        for t in range(OPERATOR_SLOTS):
            term = jnp.dot(left, held[k, t * BLOCK : (t + 1) * BLOCK, :], preferred_element_type=jnp.float32)
            if which == 0:
                acc[cols[k, t]] += term
            else:
                acc[cols[k, t]] -= term
        return carry

    lax.fori_loop(0, nblk, step, 0, unroll=4)
    for v, out in enumerate(outs):
        for b in range(out.shape[0]):
            out[b] = acc[place[3 + v] * out.shape[0] + b]


def join_kernel(place, keep, *refs):
    ins, out = refs[:4], refs[4]
    per = ins[0].shape[0]
    for v in range(4):
        spin = place[0] if v < 2 else 1 - place[0]
        row = place[1] if v % 2 == 0 else 1 - place[1]
        rows = pl.ds(pl.multiple_of(row * BLOCK, BLOCK), BLOCK)
        for b in range(per):
            value = ins[v][b]
            out[spin, rows, b * BLOCK : (b + 1) * BLOCK] = jnp.where(
                keep[row, b] > 0, value, jnp.zeros_like(value)
            )


def body(nrow, ncol, hamiltonian, metric, density, ham_keep, met_keep, dens_keep, grad_keep):
    layers, half = nrow // 2, ncol // 2
    per = ham_keep.shape[1]
    nblk = ham_keep.shape[0] * nrow
    width = per * BLOCK
    bf16, f32, i32 = jnp.bfloat16, jnp.float32, jnp.int32

    def by_row(pairs):
        return lambda a: lax.ppermute(a, "row", pairs)

    def by_mask(mask):
        return lambda a: lax.ppermute(a, "col", [(c, c ^ mask) for c in range(ncol)])

    def variant(mask):
        return (2 if mask >= half else 0) + (mask & 1)

    up = by_row([(r, (r + 2) % nrow) for r in range(nrow)])
    across = by_row([(r, r ^ 1) for r in range(nrow)])
    twin = by_mask(1)

    row, col = lax.axis_index("row").astype(i32), lax.axis_index("col").astype(i32)
    spin, part = col // half, col % 2
    z, x = row // 2, row % 2
    masks = (0, 1, half, half + 1)

    keeps = (jnp.stack([dens_keep, ham_keep, met_keep]) > 0).astype(i32)

    piece = jax.ShapeDtypeStruct((BLOCK, width), bf16)
    split = pl.pallas_call(
        split_kernel,
        out_shape=[piece] * 10,
        in_specs=[SMEM, VMEM, VMEM, VMEM],
        out_specs=[VMEM] * 10,
        cost_estimate=estimate(0, 24 * BLOCK * width * 2),
        name="split",
    )(jnp.stack([spin, part]), density, hamiltonian, metric)
    keep_rows = [lax.dynamic_index_in_dim(keeps, part ^ d, 1, keepdims=False) for d in (0, 1)]

    def exchange(pieces):
        return [pieces[0]] + [by_mask(m)(pieces[variant(m) % len(pieces)]) for m in range(1, ncol)]

    got = [exchange(p) for p in (split[:4], split[4:8], split[8:])]
    keep_got = jnp.stack(
        [keep_rows[0]] + [by_mask(m)(keep_rows[m & 1]) for m in range(1, ncol)]
    )

    slots = (DENSITY_SLOTS, OPERATOR_SLOTS, OPERATOR_SLOTS)
    packed = [
        pl.pallas_call(
            functools.partial(pack_kernel, ncol, mat, slots[mat]),
            out_shape=jax.ShapeDtypeStruct((slots[mat] * BLOCK + TAIL, BLOCK), bf16),
            in_specs=[SMEM, SMEM] + [VMEM] * ncol,
            out_specs=VMEM,
            cost_estimate=estimate(0, ncol * BLOCK * width * 2),
            name="pack",
        )(col[None], keep_got, *got[mat])
        for mat in range(3)
    ]

    gathered = [{}, {}, {}]
    curs, sides = list(packed), [None] * 3
    for t in range(layers):
        for n in range(3):
            bufs, cur, last = gathered[n], curs[n], t == layers - 1
            moves = {"side": across(cur), "twin": twin(cur)}
            if not last:
                moves["up"] = up(cur)
            if t:
                moves["back"] = twin(sides[n])
            moves = dict(zip(moves, lax.optimization_barrier(tuple(moves.values())), strict=True))
            bufs[t, 0, 0], bufs[t, 0, 1], bufs[t, 1, 0] = cur, moves["twin"], moves["side"]
            if t:
                bufs[t - 1, 1, 1] = moves["back"]
            if last:
                bufs[t, 1, 1] = twin(moves["side"])
            else:
                curs[n] = moves["up"]
            sides[n] = moves["side"]
    keys = list(gathered[0])
    place = jnp.stack([z, x, part] + [col ^ m for m in masks])

    def held(mat, extra):
        return [
            pltpu.VMEM((nblk, slots[mat] * BLOCK + TAIL, BLOCK), bf16),
            pltpu.VMEM((nblk + extra, BLOCK), i32),
            pltpu.SMEM((nblk + extra, BLOCK), i32),
            pltpu.SemaphoreType.DMA((len(keys),)),
        ]

    scratch = held(0, 8)
    prods = pl.pallas_call(
        functools.partial(first_kernel, keys, layers),
        out_shape=jax.ShapeDtypeStruct((2 * nblk, BLOCK, BLOCK), bf16),
        in_specs=[SMEM, VMEM, VMEM] + [ANY] * len(keys),
        out_specs=VMEM,
        scratch_shapes=[scratch[0], pltpu.VMEM((2 * nblk, BLOCK, BLOCK), f32)] + scratch[1:],
        cost_estimate=estimate(56 * 2 * BLOCK**3, nblk * 9 * BLOCK * BLOCK * 2),
        name="first",
    )(place, packed[1], packed[2], *[gathered[0][k] for k in keys])

    total = jax.ShapeDtypeStruct((nblk, BLOCK, BLOCK), f32)
    cost = estimate(nblk * 8 * BLOCK**3, nblk * 6 * BLOCK * BLOCK * 2)
    half_sum = pl.pallas_call(
        functools.partial(second_kernel, keys, layers, 0),
        out_shape=total,
        in_specs=[SMEM, VMEM] + [ANY] * len(keys),
        out_specs=VMEM,
        scratch_shapes=held(2, 0),
        cost_estimate=cost,
        name="second",
    )(place, prods, *[gathered[2][k] for k in keys])
    scratch = held(1, 0)
    outs = pl.pallas_call(
        functools.partial(second_kernel, keys, layers, 1),
        out_shape=[jax.ShapeDtypeStruct((per, BLOCK, BLOCK), f32)] * 4,
        in_specs=[SMEM, VMEM] + [ANY] * len(keys) + [VMEM],
        out_specs=[VMEM] * 4,
        scratch_shapes=[pltpu.VMEM((nblk, BLOCK, BLOCK), f32)] + scratch,
        cost_estimate=cost,
        name="third",
    )(place, prods, *[gathered[1][k] for k in keys], half_sum)

    back = [outs[0]] + [by_mask(m)(o) for m, o in zip(masks[1:], outs[1:], strict=True)]
    return pl.pallas_call(
        join_kernel,
        out_shape=jax.ShapeDtypeStruct((2, 2 * BLOCK, width), f32),
        in_specs=[SMEM, SMEM] + [VMEM] * 4,
        out_specs=VMEM,
        cost_estimate=estimate(0, 8 * BLOCK * width * 4),
        name="join",
    )(jnp.stack([spin, part]), grad_keep, *back)


def solution(mesh):
    grid = P("row", "col")
    spins = P(None, "row", "col")
    return jax.shard_map(
        functools.partial(body, mesh.shape["row"], mesh.shape["col"]),
        mesh=mesh,
        in_specs=(spins, grid, spins, grid, grid, grid, grid),
        out_specs=spins,
        check_vma=False,
    )
```

```python
import functools

import jax
import jax.numpy as jnp
from jax import lax
from jax.experimental import pallas as pl
from jax.experimental.pallas import tpu as pltpu
from jax.sharding import PartitionSpec as P

BLOCK = 128
OPERATOR_SLOTS = 4
DENSITY_SLOTS = 7
TAIL = 16

ANY = pl.BlockSpec(memory_space=pl.ANY)
VMEM = pl.BlockSpec(memory_space=pltpu.VMEM)
SMEM = pl.BlockSpec(memory_space=pltpu.SMEM)


def estimate(flops, nbytes):
    return pl.CostEstimate(flops=flops, bytes_accessed=nbytes, transcendentals=0)


def split_kernel(place, density, hamiltonian, metric, *outs):
    spin, row = place[0], place[1]
    for v in (2, 3, 1, 0):
        other_spin = spin if v < 2 else 1 - spin
        other_row = row if v % 2 == 0 else 1 - row
        rows = pl.ds(pl.multiple_of(other_row * BLOCK, BLOCK), BLOCK)
        outs[v][0] = density[other_spin, rows, :]
        outs[4 + v][0] = hamiltonian[other_spin, rows, :]
        outs[4 + v][1] = metric[rows, :]


def slot_rows(slot):
    start = slot * BLOCK
    return pl.ds(start if isinstance(slot, int) else pl.multiple_of(start, BLOCK), BLOCK)


def pack_kernel(sources, mats, slots, place, keep, *refs):
    ins, out = refs[:sources], refs[sources]
    per = ins[0].shape[2] // BLOCK
    here = place[4]
    lane = lax.broadcasted_iota(jnp.int32, (TAIL, BLOCK), 1)
    out[...] = jnp.zeros_like(out)
    tail = jnp.zeros((TAIL, BLOCK), jnp.int32)
    for i, mat in enumerate(mats):
        flags = [[keep[m, mat, b] for b in range(per)] for m in range(sources)]
        counts = [functools.reduce(lambda p, q: p + q, f) for f in flags]
        for m in range(sources):
            slot = jnp.int32(i * slots)
            for n in range(sources):
                if n != m:
                    slot += jnp.where((here ^ n) < (here ^ m), counts[n], 0)
            for b in range(per):

                @pl.when(flags[m][b] > 0)
                def _(slot=slot, m=m, b=b, i=i):
                    out[slot_rows(slot), :] = ins[m][i, :, b * BLOCK : (b + 1) * BLOCK]

                target = jnp.where(flags[m][b] > 0, slot, -1)
                tail = jnp.where(lane == target, (here ^ m) * per + b, tail)
                slot += flags[m][b]
    out[len(mats) * slots * BLOCK :, :] = tail.astype(jnp.float32).astype(out.dtype)


def row_of(place, key, layers):
    shift, flip, other = key
    layer = place[2] - shift
    layer = jnp.where(layer < 0, layer + layers, layer)
    side = place[3] if flip == 0 else 1 - place[3]
    half = place[1] if other == 0 else 1 - place[1]
    return (layer * 2 + side) * 2 + half


def tail_of(block):
    return block.astype(jnp.float32)[:1].astype(jnp.int32)


def parts_of(entries, layers, place, slots, bufs, tails):
    parts = []
    for n, (which, start, key) in enumerate(entries):
        view = bufs[which].at[start : start + slots * BLOCK + TAIL]
        tails[n : n + 1, :] = tail_of(view[slots * BLOCK :, :])
        parts.append((view, row_of(place, key, layers)))
    return parts


def first_kernel(entries, layers, count, place, own, *refs):
    bufs, out, acc, tails, cols = refs[:count], *refs[count:]
    nblk = len(entries)
    parts = parts_of(entries, layers, place, DENSITY_SLOTS, bufs, tails)
    tails[nblk : nblk + 1, :] = tail_of(own[2 * OPERATOR_SLOTS * BLOCK :, :])
    pltpu.sync_copy(tails, cols)
    acc[...] = jnp.zeros_like(acc)
    for i in range(2):
        mine = [cols[nblk, i * OPERATOR_SLOTS + u] for u in range(OPERATOR_SLOTS)]
        for n, (view, k) in enumerate(parts):
            slot = jnp.int32(-1)
            for u in reversed(range(OPERATOR_SLOTS)):
                slot = jnp.where(mine[u] == k, i * OPERATOR_SLOTS + u, slot)

            @pl.when(slot >= 0)
            def _(slot=slot, view=view, n=n, i=i):
                left = own[slot_rows(slot), :]
                for t in range(DENSITY_SLOTS):
                    right = view[t * BLOCK : (t + 1) * BLOCK, :]
                    acc[i * nblk + cols[n, t]] += jnp.dot(left, right, preferred_element_type=jnp.float32)

    out[...] = acc[...].astype(out.dtype)


def second_kernel(entries, layers, count, late, place, prods, *refs):
    bufs, rest = refs[:count], refs[count:]
    before = None
    if late:
        before, *outs, acc, tails, cols = rest
    else:
        acc, tails, cols = rest
        outs = ()
    nblk = acc.shape[0]
    parts = parts_of(entries, layers, place, 2 * OPERATOR_SLOTS, bufs, tails)
    pltpu.sync_copy(tails, cols)
    acc[...] = before[...] if late else jnp.zeros_like(acc)
    for n, (view, k) in enumerate(parts):
        hp, sp = prods[k], prods[nblk + k]
        for t in range(OPERATOR_SLOTS):
            u = OPERATOR_SLOTS + t
            ham, met = view[t * BLOCK : (t + 1) * BLOCK, :], view[u * BLOCK : (u + 1) * BLOCK, :]
            acc[cols[n, u]] += jnp.dot(hp, met, preferred_element_type=jnp.float32)
            acc[cols[n, t]] -= jnp.dot(sp, ham, preferred_element_type=jnp.float32)
    for v, out in enumerate(outs):
        for b in range(out.shape[0]):
            out[b] = acc[place[4 + v] * out.shape[0] + b].astype(out.dtype)


def join_kernel(place, keep, *refs):
    ins, out = refs[:4], refs[4]
    per = ins[0].shape[0]
    for v in range(4):
        spin = place[0] if v < 2 else 1 - place[0]
        row = place[1] if v % 2 == 0 else 1 - place[1]
        rows = pl.ds(pl.multiple_of(row * BLOCK, BLOCK), BLOCK)
        for b in range(per):
            value = ins[v][b].astype(out.dtype)
            out[spin, rows, b * BLOCK : (b + 1) * BLOCK] = jnp.where(
                keep[row, b] > 0, value, jnp.zeros_like(value)
            )


def body(nrow, ncol, hamiltonian, metric, density, ham_keep, met_keep, dens_keep, grad_keep):
    layers, half = nrow // 2, ncol // 2
    per = ham_keep.shape[1]
    nblk = ham_keep.shape[0] * nrow
    width = per * BLOCK
    bf16, f32, i32 = jnp.bfloat16, jnp.float32, jnp.int32

    def by_row(pairs):
        return lambda a: lax.ppermute(a, "row", pairs)

    def by_mask(mask):
        return lambda a: lax.ppermute(a, "col", [(c, c ^ mask) for c in range(ncol)])

    def variant(mask):
        return (2 if mask >= half else 0) + (mask & 1)

    up = by_row([(r, (r + 2) % nrow) for r in range(nrow)])
    across = by_row([(r, r ^ 1) for r in range(nrow)])
    twin = by_mask(1)

    row, col = lax.axis_index("row").astype(i32), lax.axis_index("col").astype(i32)
    spin, part = col // half, col % 2
    z, x = row // 2, row % 2
    masks = (0, 1, half, half + 1)

    keeps = (jnp.stack([dens_keep, ham_keep, met_keep]) > 0).astype(i32)
    place = jnp.stack([spin, part, z, x] + [col ^ m for m in masks])

    one, two = (jax.ShapeDtypeStruct((n, BLOCK, width), bf16) for n in (1, 2))
    split = pl.pallas_call(
        split_kernel,
        out_shape=[one] * 4 + [two] * 4,
        in_specs=[SMEM, VMEM, VMEM, VMEM],
        out_specs=[VMEM] * 8,
        cost_estimate=estimate(0, 24 * BLOCK * width * 2),
        name="split",
    )(place, density, hamiltonian, metric)
    keep_rows = [lax.dynamic_index_in_dim(keeps, part ^ d, 1, keepdims=False) for d in (0, 1)]

    def exchange(pieces):
        moved = {m: by_mask(m)(pieces[variant(m)]) for m in reversed(range(1, ncol))}
        return [pieces[0]] + [moved[m] for m in range(1, ncol)]

    got_dens = exchange(split[:4])
    keep_got = jnp.stack(exchange([keep_rows[0], keep_rows[1]] * 2))
    keep_got, *oper_pieces = lax.optimization_barrier((keep_got, *split[4:]))
    got_oper = exchange(oper_pieces)

    def pack(mats, slots, got):
        return pl.pallas_call(
            functools.partial(pack_kernel, ncol, mats, slots),
            out_shape=jax.ShapeDtypeStruct((len(mats) * slots * BLOCK + TAIL, BLOCK), bf16),
            in_specs=[SMEM, SMEM] + [VMEM] * ncol,
            out_specs=VMEM,
            cost_estimate=estimate(0, 8 * ncol * BLOCK * width * 2),
            name="pack",
        )(place, keep_got, *got)

    packed = [pack((0,), DENSITY_SLOTS, got_dens), pack((1, 2), OPERATOR_SLOTS, got_oper)]

    def twin_of(group):
        return twin(jnp.concatenate([a for a, _ in group], axis=0) if len(group) > 1 else group[0][0])

    gathered = [[], []]
    waiting = [[], []]
    curs = list(packed)
    for t in range(layers):
        for n in range(2):
            cur, last = curs[n], t == layers - 1
            size = cur.shape[0]

            def settle(arrived, group, n=n, size=size):
                for i, (_, key) in enumerate(group):
                    gathered[n].append((arrived, i * size, key[:2] + (1,)))

            gathered[n].append((cur, 0, (t, 0, 0)))
            waiting[n].append((cur, (t, 0, 0)))
            moves = [across(cur)] + ([] if last else [up(cur)])
            flush = waiting[n] if t % 2 == 1 or last else []
            if flush:
                moves.append(twin_of(flush))
            moves = list(lax.optimization_barrier(tuple(moves)))
            side = moves[0]
            gathered[n].append((side, 0, (t, 1, 0)))
            if flush:
                settle(moves[-1], flush)
                waiting[n] = []
            waiting[n].append((side, (t, 1, 0)))
            if last:
                settle(twin_of(waiting[n]), waiting[n])
            else:
                curs[n] = moves[1]

    def refs_of(entries):
        arrays = []
        for array, _, _ in entries:
            if not any(array is a for a in arrays):
                arrays.append(array)
        place_of = {id(a): i for i, a in enumerate(arrays)}
        return arrays, [(place_of[id(a)], start, key) for a, start, key in entries]

    arrays, entries = refs_of(gathered[0])
    tables = [pltpu.VMEM((nblk + 8, BLOCK), i32), pltpu.SMEM((nblk + 8, BLOCK), i32)]
    prods = pl.pallas_call(
        functools.partial(first_kernel, entries, layers, len(arrays)),
        out_shape=jax.ShapeDtypeStruct((2 * nblk, BLOCK, BLOCK), bf16),
        in_specs=[SMEM, VMEM] + [VMEM] * len(arrays),
        out_specs=VMEM,
        scratch_shapes=[pltpu.VMEM((2 * nblk, BLOCK, BLOCK), f32)] + tables,
        cost_estimate=estimate(56 * 2 * BLOCK**3, 10_000_000),
        name="first",
    )(place, packed[1], *arrays)

    final = (layers - 1, 1)
    early = [e for e in gathered[1] if e[2][:2] != final]
    late = [e for e in gathered[1] if e[2][:2] == final]
    tables = [pltpu.VMEM((nblk, BLOCK), i32), pltpu.SMEM((nblk, BLOCK), i32)]
    arrays, entries = refs_of(early)
    half_sum = pl.pallas_call(
        functools.partial(second_kernel, entries, layers, len(arrays), False),
        out_shape=jax.ShapeDtypeStruct((nblk, BLOCK, BLOCK), f32),
        in_specs=[SMEM, VMEM] + [VMEM] * len(arrays),
        out_specs=VMEM,
        scratch_shapes=tables,
        cost_estimate=estimate(nblk * 16 * BLOCK**3, 12_000_000),
        name="second",
    )(place, prods, *arrays)
    arrays, entries = refs_of(late)
    outs = pl.pallas_call(
        functools.partial(second_kernel, entries, layers, len(arrays), True),
        out_shape=[jax.ShapeDtypeStruct((per, BLOCK, BLOCK), f32 if m < half else bf16) for m in masks],
        in_specs=[SMEM, VMEM] + [VMEM] * len(arrays) + [VMEM],
        out_specs=[VMEM] * 4,
        scratch_shapes=[pltpu.VMEM((nblk, BLOCK, BLOCK), f32)] + tables,
        cost_estimate=estimate(4 * 8 * BLOCK**3, 6_000_000),
        name="third",
    )(place, prods, *arrays, half_sum)

    back = [outs[0]] + [by_mask(m)(o) for m, o in zip(masks[1:], outs[1:], strict=True)]
    return pl.pallas_call(
        join_kernel,
        out_shape=jax.ShapeDtypeStruct((2, 2 * BLOCK, width), f32),
        in_specs=[SMEM, SMEM] + [VMEM] * 4,
        out_specs=VMEM,
        cost_estimate=estimate(0, 8 * BLOCK * width * 4),
        name="join",
    )(place, grad_keep, *back)


def solution(mesh):
    grid = P("row", "col")
    spins = P(None, "row", "col")
    return jax.shard_map(
        functools.partial(body, mesh.shape["row"], mesh.shape["col"]),
        mesh=mesh,
        in_specs=(spins, grid, spins, grid, grid, grid, grid),
        out_specs=spins,
        check_vma=False,
    )
```

```python
import functools

import jax
import jax.numpy as jnp
from jax import lax
from jax.experimental import pallas as pl
from jax.experimental.pallas import tpu as pltpu
from jax.sharding import PartitionSpec as P

BLOCK = 128
OPERATOR_SLOTS = 4
DENSITY_SLOTS = 7
TAIL = 16

ANY = pl.BlockSpec(memory_space=pl.ANY)
VMEM = pl.BlockSpec(memory_space=pltpu.VMEM)
SMEM = pl.BlockSpec(memory_space=pltpu.SMEM)


def estimate(flops, nbytes):
    return pl.CostEstimate(flops=flops, bytes_accessed=nbytes, transcendentals=0)


def split_kernel(place, *refs):
    arrays, outs = refs[: len(refs) - 4], refs[len(refs) - 4 :]
    spin, row = place[0], place[1]
    for v in (2, 3, 1, 0):
        other_spin = spin if v < 2 else 1 - spin
        other_row = row if v % 2 == 0 else 1 - row
        rows = pl.ds(pl.multiple_of(other_row * BLOCK, BLOCK), BLOCK)
        for i, array in enumerate(arrays):
            outs[v][i] = array[rows, :] if array.ndim == 2 else array[other_spin, rows, :]


def slot_rows(slot):
    start = slot * BLOCK
    return pl.ds(start if isinstance(slot, int) else pl.multiple_of(start, BLOCK), BLOCK)


def pack_kernel(sources, mats, slots, place, keep, *refs):
    ins, out = refs[:sources], refs[sources]
    per = ins[0].shape[2] // BLOCK
    here = place[4]
    lane = lax.broadcasted_iota(jnp.int32, (TAIL, BLOCK), 1)
    out[...] = jnp.zeros_like(out)
    tail = jnp.zeros((TAIL, BLOCK), jnp.int32)
    for i, mat in enumerate(mats):
        flags = [[keep[m, mat, b] for b in range(per)] for m in range(sources)]
        counts = [functools.reduce(lambda p, q: p + q, f) for f in flags]
        for m in range(sources):
            slot = jnp.int32(i * slots)
            for n in range(sources):
                if n != m:
                    slot += jnp.where((here ^ n) < (here ^ m), counts[n], 0)
            for b in range(per):

                @pl.when(flags[m][b] > 0)
                def _(slot=slot, m=m, b=b, i=i):
                    out[slot_rows(slot), :] = ins[m][i, :, b * BLOCK : (b + 1) * BLOCK]

                target = jnp.where(flags[m][b] > 0, slot, -1)
                tail = jnp.where(lane == target, (here ^ m) * per + b, tail)
                slot += flags[m][b]
    out[len(mats) * slots * BLOCK :, :] = tail.astype(jnp.float32).astype(out.dtype)


def row_of(place, key, layers):
    shift, flip, other = key
    layer = place[2] - shift
    layer = jnp.where(layer < 0, layer + layers, layer)
    side = place[3] if flip == 0 else 1 - place[3]
    half = place[1] if other == 0 else 1 - place[1]
    return (layer * 2 + side) * 2 + half


def tail_of(block):
    return block.astype(jnp.float32)[:1].astype(jnp.int32)


def parts_of(entries, layers, place, slots, bufs, tails):
    parts = []
    for n, (which, start, key) in enumerate(entries):
        view = bufs[which].at[start : start + slots * BLOCK + TAIL]
        tails[n : n + 1, :] = tail_of(view[slots * BLOCK :, :])
        parts.append((view, row_of(place, key, layers)))
    return parts


def first_kernel(entries, layers, count, late, place, own, *refs):
    bufs, rest = refs[:count], refs[count:]
    if late:
        before, out, acc, tails, cols = rest
    else:
        acc, tails, cols = rest
    nblk, last = acc.shape[0] // 2, len(entries)
    parts = parts_of(entries, layers, place, DENSITY_SLOTS, bufs, tails)
    tails[last : last + 1, :] = tail_of(own[2 * OPERATOR_SLOTS * BLOCK :, :])
    pltpu.sync_copy(tails, cols)
    acc[...] = before[...] if late else jnp.zeros_like(acc)
    for i in range(2):
        mine = [cols[last, i * OPERATOR_SLOTS + u] for u in range(OPERATOR_SLOTS)]
        for n, (view, k) in enumerate(parts):
            slot = jnp.int32(-1)
            for u in reversed(range(OPERATOR_SLOTS)):
                slot = jnp.where(mine[u] == k, i * OPERATOR_SLOTS + u, slot)

            @pl.when(slot >= 0)
            def _(slot=slot, view=view, n=n, i=i):
                left = own[slot_rows(slot), :]
                for t in range(DENSITY_SLOTS):
                    right = view[t * BLOCK : (t + 1) * BLOCK, :]
                    acc[i * nblk + cols[n, t]] += jnp.dot(left, right, preferred_element_type=jnp.float32)

    if late:
        out[...] = acc[...].astype(out.dtype)


def second_kernel(entries, layers, count, late, place, prods, *refs):
    bufs, rest = refs[:count], refs[count:]
    if late:
        before, *outs, acc, tails, cols = rest
    else:
        acc, tails, cols = rest
        outs = ()
    nblk = acc.shape[0]
    parts = parts_of(entries, layers, place, 2 * OPERATOR_SLOTS, bufs, tails)
    pltpu.sync_copy(tails, cols)
    acc[...] = before[...] if late else jnp.zeros_like(acc)
    for n, (view, k) in enumerate(parts):
        hp, sp = prods[k], prods[nblk + k]
        for t in range(OPERATOR_SLOTS):
            u = OPERATOR_SLOTS + t
            ham, met = view[t * BLOCK : (t + 1) * BLOCK, :], view[u * BLOCK : (u + 1) * BLOCK, :]
            acc[cols[n, u]] += jnp.dot(hp, met, preferred_element_type=jnp.float32)
            acc[cols[n, t]] -= jnp.dot(sp, ham, preferred_element_type=jnp.float32)
    for v, out in enumerate(outs):
        for b in range(out.shape[0]):
            out[b] = acc[place[4 + v] * out.shape[0] + b].astype(out.dtype)


def join_kernel(place, keep, *refs):
    ins, out = refs[:4], refs[4]
    per = ins[0].shape[0]
    for v in range(4):
        spin = place[0] if v < 2 else 1 - place[0]
        row = place[1] if v % 2 == 0 else 1 - place[1]
        rows = pl.ds(pl.multiple_of(row * BLOCK, BLOCK), BLOCK)
        for b in range(per):
            value = ins[v][b].astype(out.dtype)
            out[spin, rows, b * BLOCK : (b + 1) * BLOCK] = jnp.where(
                keep[row, b] > 0, value, jnp.zeros_like(value)
            )


def body(nrow, ncol, hamiltonian, metric, density, ham_keep, met_keep, dens_keep, grad_keep):
    layers, half = nrow // 2, ncol // 2
    per = ham_keep.shape[1]
    nblk = ham_keep.shape[0] * nrow
    width = per * BLOCK
    bf16, f32, i32 = jnp.bfloat16, jnp.float32, jnp.int32

    def by_row(pairs):
        return lambda a: lax.ppermute(a, "row", pairs)

    def by_mask(mask):
        return lambda a: lax.ppermute(a, "col", [(c, c ^ mask) for c in range(ncol)])

    def variant(mask):
        return (2 if mask >= half else 0) + (mask & 1)

    up = by_row([(r, (r + 2) % nrow) for r in range(nrow)])
    across = by_row([(r, r ^ 1) for r in range(nrow)])
    twin = by_mask(1)

    row, col = lax.axis_index("row").astype(i32), lax.axis_index("col").astype(i32)
    spin, part = col // half, col % 2
    z, x = row // 2, row % 2
    masks = (0, 1, half, half + 1)

    keeps = (jnp.stack([dens_keep, ham_keep, met_keep]) > 0).astype(i32)
    place = jnp.stack([spin, part, z, x] + [col ^ m for m in masks])

    def cut(name, *arrays):
        piece = jax.ShapeDtypeStruct((len(arrays), BLOCK, width), bf16)
        return pl.pallas_call(
            split_kernel,
            out_shape=[piece] * 4,
            in_specs=[SMEM] + [VMEM] * len(arrays),
            out_specs=[VMEM] * 4,
            cost_estimate=estimate(0, 12 * len(arrays) * BLOCK * width * 2),
            name=name,
        )(place, *arrays)

    def exchange(pieces):
        moved = {m: by_mask(m)(pieces[variant(m)]) for m in reversed(range(1, ncol))}
        return [pieces[0]] + [moved[m] for m in range(1, ncol)]

    pieces = cut("cutp", density)
    keeps, *pieces = lax.optimization_barrier((keeps, *pieces))
    got_dens = exchange(pieces)
    keep_rows = [lax.dynamic_index_in_dim(keeps, part ^ d, 1, keepdims=False) for d in (0, 1)]
    keep_got = jnp.stack(exchange([keep_rows[0], keep_rows[1]] * 2))
    keep_got, hamiltonian, metric = lax.optimization_barrier((keep_got, hamiltonian, metric))
    oper_pieces = cut("cuth", hamiltonian, metric)

    def pack(mats, slots, got):
        return pl.pallas_call(
            functools.partial(pack_kernel, ncol, mats, slots),
            out_shape=jax.ShapeDtypeStruct((len(mats) * slots * BLOCK + TAIL, BLOCK), bf16),
            in_specs=[SMEM, SMEM] + [VMEM] * ncol,
            out_specs=VMEM,
            cost_estimate=estimate(0, 8 * ncol * BLOCK * width * 2),
            name="pack",
        )(place, keep_got, *got)

    dens, *oper_pieces = lax.optimization_barrier((pack((0,), DENSITY_SLOTS, got_dens), *oper_pieces))
    got_oper = exchange(oper_pieces)

    def twin_of(group):
        return twin(jnp.concatenate([a for a, _ in group], axis=0) if len(group) > 1 else group[0][0])

    def refs_of(entries):
        arrays = []
        for array, _, _ in entries:
            if not any(array is a for a in arrays):
                arrays.append(array)
        place_of = {id(a): i for i, a in enumerate(arrays)}
        return arrays, [(place_of[id(a)], start, key) for a, start, key in entries]

    final = (layers - 1, 1)
    tables = [pltpu.VMEM((2 * nblk, BLOCK), i32), pltpu.SMEM((2 * nblk, BLOCK), i32)]

    def total(n):
        return jax.ShapeDtypeStruct(((2 - n) * nblk, BLOCK, BLOCK), f32)

    def start_sum(kernel, n, given, cost, name):
        arrays, entries = refs_of([e for e in gathered[n] if e[2][:2] != final])
        return pl.pallas_call(
            functools.partial(kernel, entries, layers, len(arrays), False),
            out_shape=total(n),
            in_specs=[SMEM] + [VMEM] * (1 + len(arrays)),
            out_specs=VMEM,
            scratch_shapes=tables,
            cost_estimate=cost,
            name=name,
        )(place, given, *arrays)

    def end_sum(kernel, n, given, acc, shapes, name):
        arrays, entries = refs_of([e for e in gathered[n] if e[2][:2] == final])
        return pl.pallas_call(
            functools.partial(kernel, entries, layers, len(arrays), True),
            out_shape=shapes,
            in_specs=[SMEM] + [VMEM] * (2 + len(arrays)),
            out_specs=[VMEM] * len(shapes),
            scratch_shapes=[pltpu.VMEM(total(n).shape, f32)] + tables,
            cost_estimate=estimate(0, 6_000_000),
            name=name,
        )(place, given, *arrays, acc)

    gathered = [[], []]
    waiting = [[], []]
    curs = [dens, None]

    def settle(n, arrived, group):
        for i, (a, key) in enumerate(group):
            gathered[n].append((arrived, i * a.shape[0], key[:2] + (1,)))

    for slot in range(layers + 2):
        moves, names = [], []
        for n in range(2):
            t = slot - n
            if not 0 <= t <= layers:
                continue
            if t < layers:
                gathered[n].append((curs[n], 0, (t, 0, 0)))
                waiting[n].append((curs[n], (t, 0, 0)))
                moves.append(across(curs[n]))
                names.append((n, "side"))
            if t < layers - 1:
                moves.append(up(curs[n]))
                names.append((n, "up"))
            if t % 2 == 1 or t == layers:
                moves.append(twin_of(waiting[n]))
                settle(n, moves[-1], waiting[n])
                waiting[n] = []
                names.append((n, "twin"))
        extra = got_oper[1:] if slot == 0 else []
        if slot == layers:
            extra = [start_sum(first_kernel, 0, oper, estimate(56 * 2 * BLOCK**3, 12_000_000), "first")]
        tied = moves
        if len(moves) > 1:
            tied = lax.optimization_barrier((*moves, *extra))
            extra = tied[len(moves) :]
            tied = tied[: len(moves)]
        if slot == 0:
            oper = pack((1, 2), OPERATOR_SLOTS, [got_oper[0], *extra])
            curs[1] = oper
        if slot == layers:
            dens_sum = extra[0]
        for raw, value, (n, name) in zip(moves, tied, names, strict=True):
            if name == "up":
                curs[n] = value
            if name == "side":
                gathered[n].append((raw, 0, (slot - n, 1, 0)))
                waiting[n].append((value, (slot - n, 1, 0)))

    prods = end_sum(
        first_kernel, 0, oper, dens_sum, [jax.ShapeDtypeStruct((2 * nblk, BLOCK, BLOCK), bf16)], "firstb"
    )[0]
    oper_sum = start_sum(second_kernel, 1, prods, estimate(nblk * 16 * BLOCK**3, 12_000_000), "second")
    parts = [jax.ShapeDtypeStruct((per, BLOCK, BLOCK), f32 if m < half else bf16) for m in masks]
    outs = end_sum(second_kernel, 1, prods, oper_sum, parts, "secondb")

    back = [outs[0]] + [by_mask(m)(o) for m, o in zip(masks[1:], outs[1:], strict=True)]
    return pl.pallas_call(
        join_kernel,
        out_shape=jax.ShapeDtypeStruct((2, 2 * BLOCK, width), f32),
        in_specs=[SMEM, SMEM] + [VMEM] * 4,
        out_specs=VMEM,
        cost_estimate=estimate(0, 8 * BLOCK * width * 4),
        name="join",
    )(place, grad_keep, *back)


def solution(mesh):
    grid = P("row", "col")
    spins = P(None, "row", "col")
    return jax.shard_map(
        functools.partial(body, mesh.shape["row"], mesh.shape["col"]),
        mesh=mesh,
        in_specs=(spins, grid, spins, grid, grid, grid, grid),
        out_specs=spins,
        check_vma=False,
    )
```

```python
import functools

import jax
import jax.numpy as jnp
from jax import lax
from jax.experimental import pallas as pl
from jax.experimental.pallas import tpu as pltpu
from jax.sharding import PartitionSpec as P

BLOCK = 128
OPERATOR_SLOTS = 4
DENSITY_SLOTS = 7
TAIL = 16

ANY = pl.BlockSpec(memory_space=pl.ANY)
VMEM = pl.BlockSpec(memory_space=pltpu.VMEM)
SMEM = pl.BlockSpec(memory_space=pltpu.SMEM)


def estimate(flops, nbytes):
    return pl.CostEstimate(flops=flops, bytes_accessed=nbytes, transcendentals=0)


def split_kernel(place, dens_keep, ham_keep, met_keep, density, hamiltonian, metric, *outs):
    spin, row = place[0], place[1]
    per = dens_keep.shape[1]
    lane = lax.broadcasted_iota(jnp.int32, (TAIL, BLOCK), 1)
    for v in (2, 3, 1, 0):
        other_spin = spin if v < 2 else 1 - spin
        other_row = row if v % 2 == 0 else 1 - row
        rows = pl.ds(pl.multiple_of(other_row * BLOCK, BLOCK), BLOCK)
        outs[v][:BLOCK] = density[other_spin, rows, :]
        outs[v][BLOCK : 2 * BLOCK] = hamiltonian[other_spin, rows, :]
        outs[v][2 * BLOCK : 3 * BLOCK] = metric[rows, :]
        tail = jnp.zeros((TAIL, BLOCK), jnp.int32)
        for mat, keep in enumerate((dens_keep, ham_keep, met_keep)):
            for b in range(per):
                kept = jnp.where(keep[other_row, b] > 0, 1, 0)
                tail = jnp.where(lane == mat * per + b, kept, tail)
        outs[v][3 * BLOCK :, :BLOCK] = tail.astype(jnp.float32).astype(outs[v].dtype)
        outs[v][3 * BLOCK :, BLOCK:] = jnp.zeros((TAIL, outs[v].shape[1] - BLOCK), outs[v].dtype)


def slot_rows(slot):
    start = slot * BLOCK
    return pl.ds(start if isinstance(slot, int) else pl.multiple_of(start, BLOCK), BLOCK)


def tail_of(block):
    return block.astype(jnp.float32)[:1].astype(jnp.int32)


def pack_kernel(sources, place, *refs):
    ins, outs, (tails, keep) = refs[:sources], refs[sources : sources + 2], refs[sources + 2 :]
    per = ins[0].shape[1] // BLOCK
    here = place[4]
    for m in range(sources):
        tails[m : m + 1, :] = tail_of(ins[m][3 * BLOCK :, :BLOCK])
    pltpu.sync_copy(tails, keep)
    lane = lax.broadcasted_iota(jnp.int32, (TAIL, BLOCK), 1)
    for out, mats, slots in ((outs[0], (0,), DENSITY_SLOTS), (outs[1], (1, 2), OPERATOR_SLOTS)):
        out[...] = jnp.zeros_like(out)
        tail = jnp.zeros((TAIL, BLOCK), jnp.int32)
        for i, mat in enumerate(mats):
            flags = [[keep[m, mat * per + b] for b in range(per)] for m in range(sources)]
            counts = [functools.reduce(lambda p, q: p + q, f) for f in flags]
            for m in range(sources):
                slot = jnp.int32(i * slots)
                for n in range(sources):
                    if n != m:
                        slot += jnp.where((here ^ n) < (here ^ m), counts[n], 0)
                for b in range(per):

                    @pl.when(flags[m][b] > 0)
                    def _(slot=slot, m=m, b=b, mat=mat, out=out):
                        out[slot_rows(slot), :] = ins[m][
                            mat * BLOCK : (mat + 1) * BLOCK, b * BLOCK : (b + 1) * BLOCK
                        ]

                    target = jnp.where(flags[m][b] > 0, slot, -1)
                    tail = jnp.where(lane == target, (here ^ m) * per + b, tail)
                    slot += flags[m][b]
        out[len(mats) * slots * BLOCK :, :] = tail.astype(jnp.float32).astype(out.dtype)


def row_of(place, key, layers):
    shift, flip, other = key
    layer = place[2] - shift
    layer = jnp.where(layer < 0, layer + layers, layer)
    side = place[3] if flip == 0 else 1 - place[3]
    half = place[1] if other == 0 else 1 - place[1]
    return (layer * 2 + side) * 2 + half


def parts_of(entries, layers, place, slots, bufs, tails):
    parts = []
    for n, (which, start, key) in enumerate(entries):
        view = bufs[which].at[start : start + slots * BLOCK + TAIL]
        tails[n : n + 1, :] = tail_of(view[slots * BLOCK :, :])
        parts.append((view, row_of(place, key, layers)))
    return parts


def first_kernel(entries, layers, count, place, own, *refs):
    bufs, out, acc, tails, cols = refs[:count], *refs[count:]
    nblk = len(entries)
    parts = parts_of(entries, layers, place, DENSITY_SLOTS, bufs, tails)
    tails[nblk : nblk + 1, :] = tail_of(own[2 * OPERATOR_SLOTS * BLOCK :, :])
    pltpu.sync_copy(tails, cols)
    acc[...] = jnp.zeros_like(acc)
    for i in range(2):
        mine = [cols[nblk, i * OPERATOR_SLOTS + u] for u in range(OPERATOR_SLOTS)]
        for n, (view, k) in enumerate(parts):
            slot = jnp.int32(-1)
            for u in reversed(range(OPERATOR_SLOTS)):
                slot = jnp.where(mine[u] == k, i * OPERATOR_SLOTS + u, slot)

            @pl.when(slot >= 0)
            def _(slot=slot, view=view, n=n, i=i):
                left = own[slot_rows(slot), :]
                for t in range(DENSITY_SLOTS):
                    right = view[t * BLOCK : (t + 1) * BLOCK, :]
                    acc[i * nblk + cols[n, t]] += jnp.dot(left, right, preferred_element_type=jnp.float32)

    out[...] = acc[...].astype(out.dtype)


def second_kernel(entries, layers, count, place, prods, *refs):
    bufs, outs, (acc, tails, cols) = refs[:count], refs[count : count + 4], refs[count + 4 :]
    nblk = acc.shape[0]
    parts = parts_of(entries, layers, place, 2 * OPERATOR_SLOTS, bufs, tails)
    pltpu.sync_copy(tails, cols)
    acc[...] = jnp.zeros_like(acc)
    for n, (view, k) in enumerate(parts):
        hp, sp = prods[k], prods[nblk + k]
        for t in range(OPERATOR_SLOTS):
            u = OPERATOR_SLOTS + t
            ham, met = view[t * BLOCK : (t + 1) * BLOCK, :], view[u * BLOCK : (u + 1) * BLOCK, :]
            acc[cols[n, u]] += jnp.dot(hp, met, preferred_element_type=jnp.float32)
            acc[cols[n, t]] -= jnp.dot(sp, ham, preferred_element_type=jnp.float32)
    for v, out in enumerate(outs):
        for b in range(out.shape[0]):
            out[b] = acc[place[4 + v] * out.shape[0] + b].astype(out.dtype)


def join_kernel(place, keep, *refs):
    ins, out = refs[:4], refs[4]
    per = ins[0].shape[0]
    for v in range(4):
        spin = place[0] if v < 2 else 1 - place[0]
        row = place[1] if v % 2 == 0 else 1 - place[1]
        rows = pl.ds(pl.multiple_of(row * BLOCK, BLOCK), BLOCK)
        for b in range(per):
            value = ins[v][b].astype(out.dtype)
            out[spin, rows, b * BLOCK : (b + 1) * BLOCK] = jnp.where(
                keep[row, b] > 0, value, jnp.zeros_like(value)
            )


def body(nrow, ncol, hamiltonian, metric, density, ham_keep, met_keep, dens_keep, grad_keep):
    layers, half = nrow // 2, ncol // 2
    per = ham_keep.shape[1]
    nblk = ham_keep.shape[0] * nrow
    width = per * BLOCK
    bf16, f32, i32 = jnp.bfloat16, jnp.float32, jnp.int32

    def by_row(pairs):
        return lambda a: lax.ppermute(a, "row", pairs)

    def by_mask(mask):
        return lambda a: lax.ppermute(a, "col", [(c, c ^ mask) for c in range(ncol)])

    def variant(mask):
        return (2 if mask >= half else 0) + (mask & 1)

    up = by_row([(r, (r + 2) % nrow) for r in range(nrow)])
    across = by_row([(r, r ^ 1) for r in range(nrow)])
    twin = by_mask(1)

    row, col = lax.axis_index("row").astype(i32), lax.axis_index("col").astype(i32)
    spin, part = col // half, col % 2
    z, x = row // 2, row % 2
    masks = (0, 1, half, half + 1)

    place = jnp.stack([spin, part, z, x] + [col ^ m for m in masks])

    split = pl.pallas_call(
        split_kernel,
        out_shape=[jax.ShapeDtypeStruct((3 * BLOCK + TAIL, width), bf16)] * 4,
        in_specs=[SMEM] * 4 + [VMEM] * 3,
        out_specs=[VMEM] * 4,
        cost_estimate=estimate(0, 24 * BLOCK * width * 2),
        name="split",
    )(place, dens_keep, ham_keep, met_keep, density, hamiltonian, metric)

    def exchange(pieces):
        moved = {m: by_mask(m)(pieces[variant(m)]) for m in reversed(range(1, ncol))}
        return [pieces[0]] + [moved[m] for m in range(1, ncol)]

    got = exchange(split)

    packed = pl.pallas_call(
        functools.partial(pack_kernel, ncol),
        out_shape=[
            jax.ShapeDtypeStruct((n * BLOCK + TAIL, BLOCK), bf16) for n in (DENSITY_SLOTS, 2 * OPERATOR_SLOTS)
        ],
        in_specs=[SMEM] + [VMEM] * ncol,
        out_specs=[VMEM] * 2,
        scratch_shapes=[pltpu.VMEM((ncol, BLOCK), i32), pltpu.SMEM((ncol, BLOCK), i32)],
        cost_estimate=estimate(0, 3 * ncol * BLOCK * width * 2),
        name="pack",
    )(place, *got)

    def twin_of(group):
        return twin(jnp.concatenate([a for a, _ in group], axis=0) if len(group) > 1 else group[0][0])

    gathered = [[], []]
    waiting = [[], []]
    curs = list(packed)
    flushes = ((-1,), (-1,))
    pending = [[], []]
    for t in range(layers):
        for n in range(2):
            cur, last = curs[n], t == layers - 1
            size = cur.shape[0]

            def settle(arrived, group, n=n, size=size):
                for i, (_, key) in enumerate(group):
                    gathered[n].append((arrived, i * size, key[:2] + (1,)))

            gathered[n].append((cur, 0, (t, 0, 0)))
            waiting[n].append((cur, (t, 0, 0)))
            moves = [across(cur)] + ([] if last else [up(cur)]) + pending[n]
            pending[n] = []
            if t - layers in flushes[n]:
                arrived = twin_of(waiting[n])
                settle(arrived, waiting[n])
                waiting[n] = []
                moves.append(arrived)
            moves = lax.optimization_barrier(tuple(moves))
            side = moves[0]
            gathered[n].append((side, 0, (t, 1, 0)))
            waiting[n].append((side, (t, 1, 0)))
            if last:
                settle(twin_of(waiting[n]), waiting[n])
            else:
                curs[n] = moves[1]

    def refs_of(entries):
        arrays = []
        for array, _, _ in entries:
            if not any(array is a for a in arrays):
                arrays.append(array)
        place_of = {id(a): i for i, a in enumerate(arrays)}
        return arrays, [(place_of[id(a)], start, key) for a, start, key in entries]

    arrays, entries = refs_of(gathered[0])
    tables = [pltpu.VMEM((nblk + 8, BLOCK), i32), pltpu.SMEM((nblk + 8, BLOCK), i32)]
    prods = pl.pallas_call(
        functools.partial(first_kernel, entries, layers, len(arrays)),
        out_shape=jax.ShapeDtypeStruct((2 * nblk, BLOCK, BLOCK), bf16),
        in_specs=[SMEM, VMEM] + [VMEM] * len(arrays),
        out_specs=VMEM,
        scratch_shapes=[pltpu.VMEM((2 * nblk, BLOCK, BLOCK), f32)] + tables,
        cost_estimate=estimate(56 * 2 * BLOCK**3, 10_000_000),
        name="first",
    )(place, packed[1], *arrays)

    arrays, entries = refs_of(gathered[1])
    tables = [pltpu.VMEM((nblk, BLOCK), i32), pltpu.SMEM((nblk, BLOCK), i32)]
    outs = pl.pallas_call(
        functools.partial(second_kernel, entries, layers, len(arrays)),
        out_shape=[jax.ShapeDtypeStruct((per, BLOCK, BLOCK), f32 if m < half else bf16) for m in masks],
        in_specs=[SMEM, VMEM] + [VMEM] * len(arrays),
        out_specs=[VMEM] * 4,
        scratch_shapes=[pltpu.VMEM((nblk, BLOCK, BLOCK), f32)] + tables,
        cost_estimate=estimate(nblk * 16 * BLOCK**3, 12_000_000),
        name="second",
    )(place, prods, *arrays)

    back = [outs[0]] + [by_mask(m)(o) for m, o in zip(masks[1:], outs[1:], strict=True)]
    return pl.pallas_call(
        join_kernel,
        out_shape=jax.ShapeDtypeStruct((2, 2 * BLOCK, width), f32),
        in_specs=[SMEM, SMEM] + [VMEM] * 4,
        out_specs=VMEM,
        cost_estimate=estimate(0, 8 * BLOCK * width * 4),
        name="join",
    )(place, grad_keep, *back)


def solution(mesh):
    grid = P("row", "col")
    spins = P(None, "row", "col")
    return jax.shard_map(
        functools.partial(body, mesh.shape["row"], mesh.shape["col"]),
        mesh=mesh,
        in_specs=(spins, grid, spins, grid, grid, grid, grid),
        out_specs=spins,
        check_vma=False,
    )
```

```python
import functools

import jax
import jax.numpy as jnp
from jax import lax
from jax.experimental import pallas as pl
from jax.experimental.pallas import tpu as pltpu
from jax.sharding import PartitionSpec as P

BLOCK = 128
OPERATOR_SLOTS = 4
DENSITY_SLOTS = 7
TAIL = 16

ANY = pl.BlockSpec(memory_space=pl.ANY)
VMEM = pl.BlockSpec(memory_space=pltpu.VMEM)
SMEM = pl.BlockSpec(memory_space=pltpu.SMEM)


def estimate(flops, nbytes):
    return pl.CostEstimate(flops=flops, bytes_accessed=nbytes, transcendentals=0)


def split_kernel(place, dens_keep, ham_keep, met_keep, density, hamiltonian, metric, *outs):
    spin, row = place[0], place[1]
    per = dens_keep.shape[1]
    lane = lax.broadcasted_iota(jnp.int32, (TAIL, BLOCK), 1)
    for first, keeps in ((0, (dens_keep,)), (4, (ham_keep, met_keep))):
        for v in (2, 3, 1, 0):
            out = outs[first + v]
            other_spin = spin if v < 2 else 1 - spin
            other_row = row if v % 2 == 0 else 1 - row
            rows = pl.ds(pl.multiple_of(other_row * BLOCK, BLOCK), BLOCK)
            if first == 0:
                out[:BLOCK] = density[other_spin, rows, :]
            else:
                out[:BLOCK] = hamiltonian[other_spin, rows, :]
                out[BLOCK : 2 * BLOCK] = metric[rows, :]
            tail = jnp.zeros((TAIL, BLOCK), jnp.int32)
            for i, keep in enumerate(keeps):
                for b in range(per):
                    kept = jnp.where(keep[other_row, b] > 0, 1, 0)
                    tail = jnp.where(lane == i * per + b, kept, tail)
            end = len(keeps) * BLOCK
            out[end:, :BLOCK] = tail.astype(jnp.float32).astype(out.dtype)
            out[end:, BLOCK:] = jnp.zeros((TAIL, out.shape[1] - BLOCK), out.dtype)


def slot_rows(slot):
    start = slot * BLOCK
    return pl.ds(start if isinstance(slot, int) else pl.multiple_of(start, BLOCK), BLOCK)


def tail_of(block):
    return block.astype(jnp.float32)[:1].astype(jnp.int32)


def pack_kernel(sources, mats, slots, place, *refs):
    ins, out, (tails, keep) = refs[:sources], refs[sources], refs[sources + 1 :]
    per = ins[0].shape[1] // BLOCK
    here = place[4]
    for m in range(sources):
        tails[m : m + 1, :] = tail_of(ins[m][mats * BLOCK :, :BLOCK])
    pltpu.sync_copy(tails, keep)
    lane = lax.broadcasted_iota(jnp.int32, (TAIL, BLOCK), 1)
    out[...] = jnp.zeros_like(out)
    tail = jnp.zeros((TAIL, BLOCK), jnp.int32)
    for i in range(mats):
        flags = [[keep[m, i * per + b] for b in range(per)] for m in range(sources)]
        counts = [functools.reduce(lambda p, q: p + q, f) for f in flags]
        for m in range(sources):
            slot = jnp.int32(i * slots)
            for n in range(sources):
                if n != m:
                    slot += jnp.where((here ^ n) < (here ^ m), counts[n], 0)
            for b in range(per):

                @pl.when(flags[m][b] > 0)
                def _(slot=slot, m=m, b=b, i=i):
                    out[slot_rows(slot), :] = ins[m][i * BLOCK : (i + 1) * BLOCK, b * BLOCK : (b + 1) * BLOCK]

                target = jnp.where(flags[m][b] > 0, slot, -1)
                tail = jnp.where(lane == target, (here ^ m) * per + b, tail)
                slot += flags[m][b]
    out[mats * slots * BLOCK :, :] = tail.astype(jnp.float32).astype(out.dtype)


def row_of(place, key, layers):
    shift, flip, other = key
    layer = place[2] - shift
    layer = jnp.where(layer < 0, layer + layers, layer)
    side = place[3] if flip == 0 else 1 - place[3]
    half = place[1] if other == 0 else 1 - place[1]
    return (layer * 2 + side) * 2 + half


def parts_of(entries, layers, place, slots, bufs, tails):
    parts = []
    for n, (which, start, key) in enumerate(entries):
        view = bufs[which].at[start : start + slots * BLOCK + TAIL]
        tails[n : n + 1, :] = tail_of(view[slots * BLOCK :, :])
        parts.append((view, row_of(place, key, layers)))
    return parts


def first_kernel(entries, layers, count, place, own, *refs):
    bufs, out, acc, tails, cols = refs[:count], *refs[count:]
    nblk = len(entries)
    parts = parts_of(entries, layers, place, DENSITY_SLOTS, bufs, tails)
    tails[nblk : nblk + 1, :] = tail_of(own[2 * OPERATOR_SLOTS * BLOCK :, :])
    pltpu.sync_copy(tails, cols)
    acc[...] = jnp.zeros_like(acc)
    for i in range(2):
        mine = [cols[nblk, i * OPERATOR_SLOTS + u] for u in range(OPERATOR_SLOTS)]
        for n, (view, k) in enumerate(parts):
            slot = jnp.int32(-1)
            for u in reversed(range(OPERATOR_SLOTS)):
                slot = jnp.where(mine[u] == k, i * OPERATOR_SLOTS + u, slot)

            @pl.when(slot >= 0)
            def _(slot=slot, view=view, n=n, i=i):
                left = own[slot_rows(slot), :]
                for t in range(DENSITY_SLOTS):
                    right = view[t * BLOCK : (t + 1) * BLOCK, :]
                    acc[i * nblk + cols[n, t]] += jnp.dot(left, right, preferred_element_type=jnp.float32)

    out[...] = acc[...].astype(out.dtype)


def second_kernel(entries, layers, count, place, prods, *refs):
    bufs, outs, (acc, tails, cols) = refs[:count], refs[count : count + 4], refs[count + 4 :]
    nblk = acc.shape[0]
    parts = parts_of(entries, layers, place, 2 * OPERATOR_SLOTS, bufs, tails)
    pltpu.sync_copy(tails, cols)
    acc[...] = jnp.zeros_like(acc)
    for n, (view, k) in enumerate(parts):
        hp, sp = prods[k], prods[nblk + k]
        for t in range(OPERATOR_SLOTS):
            u = OPERATOR_SLOTS + t
            ham, met = view[t * BLOCK : (t + 1) * BLOCK, :], view[u * BLOCK : (u + 1) * BLOCK, :]
            acc[cols[n, u]] += jnp.dot(hp, met, preferred_element_type=jnp.float32)
            acc[cols[n, t]] -= jnp.dot(sp, ham, preferred_element_type=jnp.float32)
    for v, out in enumerate(outs):
        for b in range(out.shape[0]):
            out[b] = acc[place[4 + v] * out.shape[0] + b].astype(out.dtype)


def join_kernel(place, keep, *refs):
    ins, out = refs[:4], refs[4]
    per = ins[0].shape[0]
    for v in range(4):
        spin = place[0] if v < 2 else 1 - place[0]
        row = place[1] if v % 2 == 0 else 1 - place[1]
        rows = pl.ds(pl.multiple_of(row * BLOCK, BLOCK), BLOCK)
        for b in range(per):
            value = ins[v][b].astype(out.dtype)
            out[spin, rows, b * BLOCK : (b + 1) * BLOCK] = jnp.where(
                keep[row, b] > 0, value, jnp.zeros_like(value)
            )


def body(nrow, ncol, hamiltonian, metric, density, ham_keep, met_keep, dens_keep, grad_keep):
    layers, half = nrow // 2, ncol // 2
    per = ham_keep.shape[1]
    nblk = ham_keep.shape[0] * nrow
    width = per * BLOCK
    bf16, f32, i32 = jnp.bfloat16, jnp.float32, jnp.int32

    def by_row(pairs):
        return lambda a: lax.ppermute(a, "row", pairs)

    def by_mask(mask):
        return lambda a: lax.ppermute(a, "col", [(c, c ^ mask) for c in range(ncol)])

    def variant(mask):
        return (2 if mask >= half else 0) + (mask & 1)

    up = by_row([(r, (r + 2) % nrow) for r in range(nrow)])
    across = by_row([(r, r ^ 1) for r in range(nrow)])
    twin = by_mask(1)

    row, col = lax.axis_index("row").astype(i32), lax.axis_index("col").astype(i32)
    spin, part = col // half, col % 2
    z, x = row // 2, row % 2
    masks = (0, 1, half, half + 1)

    place = jnp.stack([spin, part, z, x] + [col ^ m for m in masks])

    split = pl.pallas_call(
        split_kernel,
        out_shape=[jax.ShapeDtypeStruct((n * BLOCK + TAIL, width), bf16) for n in (1, 1, 1, 1, 2, 2, 2, 2)],
        in_specs=[SMEM] * 4 + [VMEM] * 3,
        out_specs=[VMEM] * 8,
        cost_estimate=estimate(0, 24 * BLOCK * width * 2),
        name="split",
    )(place, dens_keep, ham_keep, met_keep, density, hamiltonian, metric)

    def exchange(pieces):
        moved = {m: by_mask(m)(pieces[variant(m)]) for m in reversed(range(1, ncol))}
        return [pieces[0]] + [moved[m] for m in range(1, ncol)]

    got_dens = exchange(split[:4])
    got_dens[1], *oper_pieces = lax.optimization_barrier((got_dens[1], *split[4:]))
    got_oper = exchange(oper_pieces)

    def pack(mats, slots, got):
        return pl.pallas_call(
            functools.partial(pack_kernel, ncol, mats, slots),
            out_shape=jax.ShapeDtypeStruct((mats * slots * BLOCK + TAIL, BLOCK), bf16),
            in_specs=[SMEM] + [VMEM] * ncol,
            out_specs=VMEM,
            scratch_shapes=[pltpu.VMEM((ncol, BLOCK), i32), pltpu.SMEM((ncol, BLOCK), i32)],
            cost_estimate=estimate(0, 3 * ncol * BLOCK * width * 2),
            name="pack",
        )(place, *got)

    packed = [pack(1, DENSITY_SLOTS, got_dens), pack(2, OPERATOR_SLOTS, got_oper)]

    def twin_of(group):
        return twin(jnp.concatenate([a for a, _ in group], axis=0) if len(group) > 1 else group[0][0])

    def refs_of(entries):
        arrays = []
        for array, _, _ in entries:
            if not any(array is a for a in arrays):
                arrays.append(array)
        place_of = {id(a): i for i, a in enumerate(arrays)}
        return arrays, [(place_of[id(a)], start, key) for a, start, key in entries]

    gathered = [[], []]
    waiting = [[], []]
    curs = list(packed)
    def first_product():
        arrays, entries = refs_of(gathered[0])
        tables = [pltpu.VMEM((nblk + 8, BLOCK), i32), pltpu.SMEM((nblk + 8, BLOCK), i32)]
        return pl.pallas_call(
            functools.partial(first_kernel, entries, layers, len(arrays)),
            out_shape=jax.ShapeDtypeStruct((2 * nblk, BLOCK, BLOCK), bf16),
            in_specs=[SMEM, VMEM] + [VMEM] * len(arrays),
            out_specs=VMEM,
            scratch_shapes=[pltpu.VMEM((2 * nblk, BLOCK, BLOCK), f32)] + tables,
            cost_estimate=estimate(56 * 2 * BLOCK**3, 10_000_000),
            name="first",
        )(place, packed[1], *arrays)

    def settle(n, group, joined=None):
        arrived = twin_of(group) if joined is None else twin(joined)
        for i, (a, key) in enumerate(group):
            gathered[n].append((arrived, i * a.shape[0], key[:2] + (1,)))
        return arrived

    joined = [None, None]

    def advance(n, t, extra=()):
        cur, last = curs[n], t == layers - 1
        gathered[n].append((cur, 0, (t, 0, 0)))
        waiting[n].append((cur, (t, 0, 0)))
        moves = [across(cur)]
        if last:
            early, pair = waiting[n][:-2], waiting[n][-2:]
            moves.append(settle(n, early, joined[n]))
            moves += ([settle(n, pair)] if n == 0 else [settle(n, [one]) for one in pair])
        else:
            moves.append(up(cur))
            if t == layers - 2:
                moves.append(jnp.concatenate([a for a, _ in waiting[n]], axis=0))
        tied = lax.optimization_barrier((*moves, *extra))
        side = tied[0]
        gathered[n].append((side, 0, (t, 1, 0)))
        if last:
            settle(n, [(side, (t, 1, 0))])
        else:
            waiting[n].append((side, (t, 1, 0)))
            curs[n] = tied[1]
            if t == layers - 2:
                joined[n] = tied[2]
        return list(tied[: len(moves)]), list(tied[len(moves) :])

    ahead, _ = advance(0, 0)
    for t in range(layers):
        if t < layers - 1:
            ahead, _ = advance(0, t + 1)
            advance(1, t, ahead)
        else:
            prods = advance(1, t, [first_product()])[1][0]

    arrays, entries = refs_of(gathered[1])
    tables = [pltpu.VMEM((nblk, BLOCK), i32), pltpu.SMEM((nblk, BLOCK), i32)]
    outs = pl.pallas_call(
        functools.partial(second_kernel, entries, layers, len(arrays)),
        out_shape=[jax.ShapeDtypeStruct((per, BLOCK, BLOCK), f32 if m < half else bf16) for m in masks],
        in_specs=[SMEM, VMEM] + [VMEM] * len(arrays),
        out_specs=[VMEM] * 4,
        scratch_shapes=[pltpu.VMEM((nblk, BLOCK, BLOCK), f32)] + tables,
        cost_estimate=estimate(nblk * 16 * BLOCK**3, 12_000_000),
        name="second",
    )(place, prods, *arrays)

    back = [outs[0]] + [by_mask(m)(o) for m, o in zip(masks[1:], outs[1:], strict=True)]
    return pl.pallas_call(
        join_kernel,
        out_shape=jax.ShapeDtypeStruct((2, 2 * BLOCK, width), f32),
        in_specs=[SMEM, SMEM] + [VMEM] * 4,
        out_specs=VMEM,
        cost_estimate=estimate(0, 8 * BLOCK * width * 4),
        name="join",
    )(place, grad_keep, *back)


def solution(mesh):
    grid = P("row", "col")
    spins = P(None, "row", "col")
    return jax.shard_map(
        functools.partial(body, mesh.shape["row"], mesh.shape["col"]),
        mesh=mesh,
        in_specs=(spins, grid, spins, grid, grid, grid, grid),
        out_specs=spins,
        check_vma=False,
    )
```

```python
import functools

import jax
import jax.numpy as jnp
from jax import lax
from jax.experimental import pallas as pl
from jax.experimental.pallas import tpu as pltpu
from jax.sharding import PartitionSpec as P

BLOCK = 128
OPERATOR_SLOTS = 4
DENSITY_SLOTS = 7
TAIL = 16

ANY = pl.BlockSpec(memory_space=pl.ANY)
VMEM = pl.BlockSpec(memory_space=pltpu.VMEM)
SMEM = pl.BlockSpec(memory_space=pltpu.SMEM)


def estimate(flops, nbytes):
    return pl.CostEstimate(flops=flops, bytes_accessed=nbytes, transcendentals=0)


def split_kernel(place, dens_keep, ham_keep, met_keep, density, hamiltonian, metric, *outs):
    spin, row = place[0], place[1]
    per = dens_keep.shape[1]
    lane = lax.broadcasted_iota(jnp.int32, (TAIL, BLOCK), 1)
    for first, keeps in ((0, (dens_keep,)), (4, (ham_keep, met_keep))):
        for v in (2, 3, 1, 0):
            out = outs[first + v]
            other_spin = spin if v < 2 else 1 - spin
            other_row = row if v % 2 == 0 else 1 - row
            rows = pl.ds(pl.multiple_of(other_row * BLOCK, BLOCK), BLOCK)
            if first == 0:
                out[:BLOCK] = density[other_spin, rows, :]
            else:
                out[:BLOCK] = hamiltonian[other_spin, rows, :]
                out[BLOCK : 2 * BLOCK] = metric[rows, :]
            tail = jnp.zeros((TAIL, BLOCK), jnp.int32)
            for i, keep in enumerate(keeps):
                for b in range(per):
                    kept = jnp.where(keep[other_row, b] > 0, 1, 0)
                    tail = jnp.where(lane == i * per + b, kept, tail)
            end = len(keeps) * BLOCK
            out[end:, :BLOCK] = tail.astype(jnp.float32).astype(out.dtype)
            out[end:, BLOCK:] = jnp.zeros((TAIL, out.shape[1] - BLOCK), out.dtype)


def slot_rows(slot):
    start = slot * BLOCK
    return pl.ds(start if isinstance(slot, int) else pl.multiple_of(start, BLOCK), BLOCK)


def tail_of(block):
    return block.astype(jnp.float32)[:1].astype(jnp.int32)


def pack_kernel(sources, mats, slots, place, *refs):
    ins, out, (tails, keep) = refs[:sources], refs[sources], refs[sources + 1 :]
    per = ins[0].shape[1] // BLOCK
    here = place[4]
    for m in range(sources):
        tails[m : m + 1, :] = tail_of(ins[m][mats * BLOCK :, :BLOCK])
    pltpu.sync_copy(tails, keep)
    lane = lax.broadcasted_iota(jnp.int32, (TAIL, BLOCK), 1)
    out[...] = jnp.zeros_like(out)
    tail = jnp.zeros((TAIL, BLOCK), jnp.int32)
    for i in range(mats):
        flags = [[keep[m, i * per + b] for b in range(per)] for m in range(sources)]
        counts = [functools.reduce(lambda p, q: p + q, f) for f in flags]
        for m in range(sources):
            slot = jnp.int32(i * slots)
            for n in range(sources):
                if n != m:
                    slot += jnp.where((here ^ n) < (here ^ m), counts[n], 0)
            for b in range(per):

                @pl.when(flags[m][b] > 0)
                def _(slot=slot, m=m, b=b, i=i):
                    out[slot_rows(slot), :] = ins[m][i * BLOCK : (i + 1) * BLOCK, b * BLOCK : (b + 1) * BLOCK]

                target = jnp.where(flags[m][b] > 0, slot, -1)
                tail = jnp.where(lane == target, (here ^ m) * per + b, tail)
                slot += flags[m][b]
    out[mats * slots * BLOCK :, :] = tail.astype(jnp.float32).astype(out.dtype)


def row_of(place, key, layers):
    shift, flip, other = key
    layer = place[2] - shift
    layer = jnp.where(layer < 0, layer + layers, layer)
    side = place[3] if flip == 0 else 1 - place[3]
    half = place[1] if other == 0 else 1 - place[1]
    return (layer * 2 + side) * 2 + half


def parts_of(entries, layers, place, slots, bufs, tails):
    parts = []
    for n, (which, start, key) in enumerate(entries):
        view = bufs[which].at[start : start + slots * BLOCK + TAIL]
        tails[n : n + 1, :] = tail_of(view[slots * BLOCK :, :])
        parts.append((view, row_of(place, key, layers)))
    return parts


def first_kernel(entries, layers, count, place, own, *refs):
    bufs, out, acc, tails, cols = refs[:count], *refs[count:]
    nblk = len(entries)
    parts = parts_of(entries, layers, place, DENSITY_SLOTS, bufs, tails)
    tails[nblk : nblk + 1, :] = tail_of(own[2 * OPERATOR_SLOTS * BLOCK :, :])
    pltpu.sync_copy(tails, cols)
    acc[...] = jnp.zeros_like(acc)
    for i in range(2):
        mine = [cols[nblk, i * OPERATOR_SLOTS + u] for u in range(OPERATOR_SLOTS)]
        for n, (view, k) in enumerate(parts):
            slot = jnp.int32(-1)
            for u in reversed(range(OPERATOR_SLOTS)):
                slot = jnp.where(mine[u] == k, i * OPERATOR_SLOTS + u, slot)

            @pl.when(slot >= 0)
            def _(slot=slot, view=view, n=n, i=i):
                left = own[slot_rows(slot), :]
                for t in range(DENSITY_SLOTS):
                    right = view[t * BLOCK : (t + 1) * BLOCK, :]
                    acc[i * nblk + cols[n, t]] += jnp.dot(left, right, preferred_element_type=jnp.float32)

    out[...] = acc[...].astype(out.dtype)


def second_kernel(entries, layers, count, place, prods, *refs):
    bufs, outs, (acc, tails, cols) = refs[:count], refs[count : count + 4], refs[count + 4 :]
    nblk = acc.shape[0]
    parts = parts_of(entries, layers, place, 2 * OPERATOR_SLOTS, bufs, tails)
    pltpu.sync_copy(tails, cols)
    acc[...] = jnp.zeros_like(acc)
    for n, (view, k) in enumerate(parts):
        hp, sp = prods[k], prods[nblk + k]
        for t in range(OPERATOR_SLOTS):
            u = OPERATOR_SLOTS + t
            ham, met = view[t * BLOCK : (t + 1) * BLOCK, :], view[u * BLOCK : (u + 1) * BLOCK, :]
            acc[cols[n, u]] += jnp.dot(hp, met, preferred_element_type=jnp.float32)
            acc[cols[n, t]] -= jnp.dot(sp, ham, preferred_element_type=jnp.float32)
    for v, out in enumerate(outs):
        for b in range(out.shape[0]):
            out[b] = acc[place[4 + v] * out.shape[0] + b].astype(out.dtype)


def join_kernel(place, keep, *refs):
    ins, out = refs[:4], refs[4]
    per = ins[0].shape[0]
    for v in range(4):
        spin = place[0] if v < 2 else 1 - place[0]
        row = place[1] if v % 2 == 0 else 1 - place[1]
        rows = pl.ds(pl.multiple_of(row * BLOCK, BLOCK), BLOCK)
        for b in range(per):
            value = ins[v][b].astype(out.dtype)
            out[spin, rows, b * BLOCK : (b + 1) * BLOCK] = jnp.where(
                keep[row, b] > 0, value, jnp.zeros_like(value)
            )


def body(nrow, ncol, hamiltonian, metric, density, ham_keep, met_keep, dens_keep, grad_keep):
    layers, half = nrow // 2, ncol // 2
    per = ham_keep.shape[1]
    nblk = ham_keep.shape[0] * nrow
    width = per * BLOCK
    bf16, f32, i32 = jnp.bfloat16, jnp.float32, jnp.int32

    def by_row(pairs):
        return lambda a: lax.ppermute(a, "row", pairs)

    def by_mask(mask):
        return lambda a: lax.ppermute(a, "col", [(c, c ^ mask) for c in range(ncol)])

    def variant(mask):
        return (2 if mask >= half else 0) + (mask & 1)

    up = by_row([(r, (r + 2) % nrow) for r in range(nrow)])
    across = by_row([(r, r ^ 1) for r in range(nrow)])
    twin = by_mask(1)

    row, col = lax.axis_index("row").astype(i32), lax.axis_index("col").astype(i32)
    spin, part = col // half, col % 2
    z, x = row // 2, row % 2
    masks = (0, 1, half, half + 1)

    place = jnp.stack([spin, part, z, x] + [col ^ m for m in masks])

    split = pl.pallas_call(
        split_kernel,
        out_shape=[jax.ShapeDtypeStruct((n * BLOCK + TAIL, width), bf16) for n in (1, 1, 1, 1, 2, 2, 2, 2)],
        in_specs=[SMEM] * 4 + [VMEM] * 3,
        out_specs=[VMEM] * 8,
        cost_estimate=estimate(0, 24 * BLOCK * width * 2),
        name="split",
    )(place, dens_keep, ham_keep, met_keep, density, hamiltonian, metric)

    def exchange(pieces):
        moved = {m: by_mask(m)(pieces[variant(m)]) for m in reversed(range(1, ncol))}
        return [pieces[0]] + [moved[m] for m in range(1, ncol)]

    got_dens = exchange(split[:4])
    got_dens[half], *oper_pieces = lax.optimization_barrier((got_dens[half], *split[4:]))
    got_oper = exchange(oper_pieces)

    def pack(mats, slots, got):
        return pl.pallas_call(
            functools.partial(pack_kernel, ncol, mats, slots),
            out_shape=jax.ShapeDtypeStruct((mats * slots * BLOCK + TAIL, BLOCK), bf16),
            in_specs=[SMEM] + [VMEM] * ncol,
            out_specs=VMEM,
            scratch_shapes=[pltpu.VMEM((ncol, BLOCK), i32), pltpu.SMEM((ncol, BLOCK), i32)],
            cost_estimate=estimate(0, 3 * ncol * BLOCK * width * 2),
            name="pack",
        )(place, *got)

    packed = [pack(1, DENSITY_SLOTS, got_dens), pack(2, OPERATOR_SLOTS, got_oper)]

    def twin_of(group):
        return twin(jnp.concatenate([a for a, _ in group], axis=0) if len(group) > 1 else group[0][0])

    def refs_of(entries):
        arrays = []
        for array, _, _ in entries:
            if not any(array is a for a in arrays):
                arrays.append(array)
        place_of = {id(a): i for i, a in enumerate(arrays)}
        return arrays, [(place_of[id(a)], start, key) for a, start, key in entries]

    gathered = [[], []]
    waiting = [[], []]
    curs = list(packed)
    def first_product():
        arrays, entries = refs_of(gathered[0])
        tables = [pltpu.VMEM((nblk + 8, BLOCK), i32), pltpu.SMEM((nblk + 8, BLOCK), i32)]
        return pl.pallas_call(
            functools.partial(first_kernel, entries, layers, len(arrays)),
            out_shape=jax.ShapeDtypeStruct((2 * nblk, BLOCK, BLOCK), bf16),
            in_specs=[SMEM, VMEM] + [VMEM] * len(arrays),
            out_specs=VMEM,
            scratch_shapes=[pltpu.VMEM((2 * nblk, BLOCK, BLOCK), f32)] + tables,
            cost_estimate=estimate(56 * 2 * BLOCK**3, 10_000_000),
            name="first",
        )(place, packed[1], *arrays)

    def settle(n, group, joined=None):
        arrived = twin_of(group) if joined is None else twin(joined)
        for i, (a, key) in enumerate(group):
            gathered[n].append((arrived, i * a.shape[0], key[:2] + (1,)))
        return arrived

    joined = [None, None]

    def advance(n, t, extra=()):
        cur, last = curs[n], t == layers - 1
        gathered[n].append((cur, 0, (t, 0, 0)))
        waiting[n].append((cur, (t, 0, 0)))
        moves = [across(cur)]
        if last:
            early, pair = waiting[n][:-2], waiting[n][-2:]
            moves.append(settle(n, early, joined[n]))
            moves += ([settle(n, pair)] if n == 0 else [settle(n, [one]) for one in pair])
        else:
            moves.append(up(cur))
            if t == layers - 2:
                moves.append(jnp.concatenate([a for a, _ in waiting[n]], axis=0))
        tied = lax.optimization_barrier((*moves, *extra))
        side = tied[0]
        gathered[n].append((side, 0, (t, 1, 0)))
        if last:
            settle(n, [(side, (t, 1, 0))])
        else:
            waiting[n].append((side, (t, 1, 0)))
            curs[n] = tied[1]
            if t == layers - 2:
                joined[n] = tied[2]
        return list(tied[: len(moves)]), list(tied[len(moves) :])

    ahead, _ = advance(0, 0)
    for t in range(layers):
        if t < layers - 1:
            ahead, _ = advance(0, t + 1)
            advance(1, t, ahead[:1])
        else:
            prods = advance(1, t, [first_product()])[1][0]

    arrays, entries = refs_of(gathered[1])
    tables = [pltpu.VMEM((nblk, BLOCK), i32), pltpu.SMEM((nblk, BLOCK), i32)]
    outs = pl.pallas_call(
        functools.partial(second_kernel, entries, layers, len(arrays)),
        out_shape=[jax.ShapeDtypeStruct((per, BLOCK, BLOCK), f32 if m < half else bf16) for m in masks],
        in_specs=[SMEM, VMEM] + [VMEM] * len(arrays),
        out_specs=[VMEM] * 4,
        scratch_shapes=[pltpu.VMEM((nblk, BLOCK, BLOCK), f32)] + tables,
        cost_estimate=estimate(nblk * 16 * BLOCK**3, 12_000_000),
        name="second",
    )(place, prods, *arrays)

    back = [outs[0]] + [by_mask(m)(o) for m, o in zip(masks[1:], outs[1:], strict=True)]
    return pl.pallas_call(
        join_kernel,
        out_shape=jax.ShapeDtypeStruct((2, 2 * BLOCK, width), f32),
        in_specs=[SMEM, SMEM] + [VMEM] * 4,
        out_specs=VMEM,
        cost_estimate=estimate(0, 8 * BLOCK * width * 4),
        name="join",
    )(place, grad_keep, *back)


def solution(mesh):
    grid = P("row", "col")
    spins = P(None, "row", "col")
    return jax.shard_map(
        functools.partial(body, mesh.shape["row"], mesh.shape["col"]),
        mesh=mesh,
        in_specs=(spins, grid, spins, grid, grid, grid, grid),
        out_specs=spins,
        check_vma=False,
    )
```

```python
import functools

import jax
import jax.numpy as jnp
from jax import lax
from jax.experimental import pallas as pl
from jax.experimental.pallas import tpu as pltpu
from jax.sharding import PartitionSpec as P

BLOCK = 128
OPERATOR_SLOTS = 4
DENSITY_SLOTS = 7
TAIL = 16

ANY = pl.BlockSpec(memory_space=pl.ANY)
VMEM = pl.BlockSpec(memory_space=pltpu.VMEM)
SMEM = pl.BlockSpec(memory_space=pltpu.SMEM)


def estimate(flops, nbytes):
    return pl.CostEstimate(flops=flops, bytes_accessed=nbytes, transcendentals=0)


def split_kernel(half, dens_keep, ham_keep, met_keep, density, hamiltonian, metric, *outs):
    col = lax.axis_index("col")
    spin, row = jnp.where(col >= half, 1, 0), lax.rem(col, 2)
    per = dens_keep.shape[1]
    lane = lax.broadcasted_iota(jnp.int32, (TAIL, BLOCK), 1)
    for first, keeps in ((0, (dens_keep,)), (4, (ham_keep, met_keep))):
        for v in (2, 3, 1, 0):
            out = outs[first + v]
            other_spin = spin if v < 2 else 1 - spin
            other_row = row if v % 2 == 0 else 1 - row
            rows = pl.ds(pl.multiple_of(other_row * BLOCK, BLOCK), BLOCK)
            if first == 0:
                out[:BLOCK] = density[other_spin, rows, :]
            else:
                out[:BLOCK] = hamiltonian[other_spin, rows, :]
                out[BLOCK : 2 * BLOCK] = metric[rows, :]
            tail = jnp.zeros((TAIL, BLOCK), jnp.int32)
            for i, keep in enumerate(keeps):
                for b in range(per):
                    kept = jnp.where(keep[other_row, b] > 0, 1, 0)
                    tail = jnp.where(lane == i * per + b, kept, tail)
            end = len(keeps) * BLOCK
            out[end:, :BLOCK] = tail.astype(jnp.float32).astype(out.dtype)
            out[end:, BLOCK:] = jnp.zeros((TAIL, out.shape[1] - BLOCK), out.dtype)


def slot_rows(slot):
    start = slot * BLOCK
    return pl.ds(start if isinstance(slot, int) else pl.multiple_of(start, BLOCK), BLOCK)


def tail_of(block):
    return block.astype(jnp.float32)[:1].astype(jnp.int32)


def pack_kernel(sources, mats, slots, place, *refs):
    ins, out, (tails, keep) = refs[:sources], refs[sources], refs[sources + 1 :]
    per = ins[0].shape[1] // BLOCK
    here = place[4]
    for m in range(sources):
        tails[m : m + 1, :] = tail_of(ins[m][mats * BLOCK :, :BLOCK])
    pltpu.sync_copy(tails, keep)
    lane = lax.broadcasted_iota(jnp.int32, (TAIL, BLOCK), 1)
    out[...] = jnp.zeros_like(out)
    tail = jnp.zeros((TAIL, BLOCK), jnp.int32)
    for i in range(mats):
        flags = [[keep[m, i * per + b] for b in range(per)] for m in range(sources)]
        counts = [functools.reduce(lambda p, q: p + q, f) for f in flags]
        for m in range(sources):
            slot = jnp.int32(i * slots)
            for n in range(sources):
                if n != m:
                    slot += jnp.where((here ^ n) < (here ^ m), counts[n], 0)
            for b in range(per):

                @pl.when(flags[m][b] > 0)
                def _(slot=slot, m=m, b=b, i=i):
                    out[slot_rows(slot), :] = ins[m][i * BLOCK : (i + 1) * BLOCK, b * BLOCK : (b + 1) * BLOCK]

                target = jnp.where(flags[m][b] > 0, slot, -1)
                tail = jnp.where(lane == target, (here ^ m) * per + b, tail)
                slot += flags[m][b]
    out[mats * slots * BLOCK :, :] = tail.astype(jnp.float32).astype(out.dtype)


def row_of(place, key, layers):
    shift, flip, other = key
    layer = place[2] - shift
    layer = jnp.where(layer < 0, layer + layers, layer)
    side = place[3] if flip == 0 else 1 - place[3]
    half = place[1] if other == 0 else 1 - place[1]
    return (layer * 2 + side) * 2 + half


def parts_of(entries, layers, place, slots, bufs, tails):
    parts = []
    for n, (which, start, key) in enumerate(entries):
        view = bufs[which].at[start : start + slots * BLOCK + TAIL]
        tails[n : n + 1, :] = tail_of(view[slots * BLOCK :, :])
        parts.append((view, row_of(place, key, layers)))
    return parts


def first_kernel(entries, layers, count, place, own, *refs):
    bufs, out, acc, tails, cols = refs[:count], *refs[count:]
    nblk = len(entries)
    parts = parts_of(entries, layers, place, DENSITY_SLOTS, bufs, tails)
    tails[nblk : nblk + 1, :] = tail_of(own[2 * OPERATOR_SLOTS * BLOCK :, :])
    pltpu.sync_copy(tails, cols)
    acc[...] = jnp.zeros_like(acc)
    for i in range(2):
        mine = [cols[nblk, i * OPERATOR_SLOTS + u] for u in range(OPERATOR_SLOTS)]
        for n, (view, k) in enumerate(parts):
            slot = jnp.int32(-1)
            for u in reversed(range(OPERATOR_SLOTS)):
                slot = jnp.where(mine[u] == k, i * OPERATOR_SLOTS + u, slot)

            @pl.when(slot >= 0)
            def _(slot=slot, view=view, n=n, i=i):
                left = own[slot_rows(slot), :]
                for t in range(DENSITY_SLOTS):
                    right = view[t * BLOCK : (t + 1) * BLOCK, :]
                    acc[i * nblk + cols[n, t]] += jnp.dot(left, right, preferred_element_type=jnp.float32)

    out[...] = acc[...].astype(out.dtype)


def second_kernel(entries, layers, count, place, prods, *refs):
    bufs, outs, (acc, tails, cols) = refs[:count], refs[count : count + 4], refs[count + 4 :]
    nblk = acc.shape[0]
    parts = parts_of(entries, layers, place, 2 * OPERATOR_SLOTS, bufs, tails)
    pltpu.sync_copy(tails, cols)
    acc[...] = jnp.zeros_like(acc)
    for n, (view, k) in enumerate(parts):
        hp, sp = prods[k], prods[nblk + k]
        for t in range(OPERATOR_SLOTS):
            u = OPERATOR_SLOTS + t
            ham, met = view[t * BLOCK : (t + 1) * BLOCK, :], view[u * BLOCK : (u + 1) * BLOCK, :]
            acc[cols[n, u]] += jnp.dot(hp, met, preferred_element_type=jnp.float32)
            acc[cols[n, t]] -= jnp.dot(sp, ham, preferred_element_type=jnp.float32)
    for v, out in enumerate(outs):
        for b in range(out.shape[0]):
            out[b] = acc[place[4 + v] * out.shape[0] + b].astype(out.dtype)


def join_kernel(place, keep, *refs):
    ins, out = refs[:4], refs[4]
    per = ins[0].shape[0]
    for v in range(4):
        spin = place[0] if v < 2 else 1 - place[0]
        row = place[1] if v % 2 == 0 else 1 - place[1]
        rows = pl.ds(pl.multiple_of(row * BLOCK, BLOCK), BLOCK)
        for b in range(per):
            value = ins[v][b].astype(out.dtype)
            out[spin, rows, b * BLOCK : (b + 1) * BLOCK] = jnp.where(
                keep[row, b] > 0, value, jnp.zeros_like(value)
            )


def body(nrow, ncol, hamiltonian, metric, density, ham_keep, met_keep, dens_keep, grad_keep):
    layers, half = nrow // 2, ncol // 2
    per = ham_keep.shape[1]
    nblk = ham_keep.shape[0] * nrow
    width = per * BLOCK
    bf16, f32, i32 = jnp.bfloat16, jnp.float32, jnp.int32

    def by_row(pairs):
        return lambda a: lax.ppermute(a, "row", pairs)

    def by_mask(mask):
        return lambda a: lax.ppermute(a, "col", [(c, c ^ mask) for c in range(ncol)])

    def variant(mask):
        return (2 if mask >= half else 0) + (mask & 1)

    up = by_row([(r, (r + 2) % nrow) for r in range(nrow)])
    across = by_row([(r, r ^ 1) for r in range(nrow)])
    twin = by_mask(1)

    row, col = lax.axis_index("row").astype(i32), lax.axis_index("col").astype(i32)
    spin, part = col // half, col % 2
    z, x = row // 2, row % 2
    masks = (0, 1, half, half + 1)

    place = jnp.stack([spin, part, z, x] + [col ^ m for m in masks])

    split = pl.pallas_call(
        functools.partial(split_kernel, half),
        out_shape=[jax.ShapeDtypeStruct((n * BLOCK + TAIL, width), bf16) for n in (1, 1, 1, 1, 2, 2, 2, 2)],
        in_specs=[SMEM] * 3 + [VMEM] * 3,
        out_specs=[VMEM] * 8,
        cost_estimate=estimate(0, 24 * BLOCK * width * 2),
        name="split",
    )(dens_keep, ham_keep, met_keep, density, hamiltonian, metric)

    def exchange(pieces):
        moved = {m: by_mask(m)(pieces[variant(m)]) for m in reversed(range(1, ncol))}
        return [pieces[0]] + [moved[m] for m in range(1, ncol)]

    got_dens = exchange(split[:4])
    got_dens[half], *oper_pieces = lax.optimization_barrier((got_dens[half], *split[4:]))
    got_oper = exchange(oper_pieces)

    def pack(mats, slots, got):
        return pl.pallas_call(
            functools.partial(pack_kernel, ncol, mats, slots),
            out_shape=jax.ShapeDtypeStruct((mats * slots * BLOCK + TAIL, BLOCK), bf16),
            in_specs=[SMEM] + [VMEM] * ncol,
            out_specs=VMEM,
            scratch_shapes=[pltpu.VMEM((ncol, BLOCK), i32), pltpu.SMEM((ncol, BLOCK), i32)],
            cost_estimate=estimate(0, 3 * ncol * BLOCK * width * 2),
            name="pack",
        )(place, *got)

    packed = [pack(1, DENSITY_SLOTS, got_dens), pack(2, OPERATOR_SLOTS, got_oper)]

    def twin_of(group):
        return twin(jnp.concatenate([a for a, _ in group], axis=0) if len(group) > 1 else group[0][0])

    def refs_of(entries):
        arrays = []
        for array, _, _ in entries:
            if not any(array is a for a in arrays):
                arrays.append(array)
        place_of = {id(a): i for i, a in enumerate(arrays)}
        return arrays, [(place_of[id(a)], start, key) for a, start, key in entries]

    gathered = [[], []]
    waiting = [[], []]
    curs = list(packed)
    def first_product():
        arrays, entries = refs_of(gathered[0])
        tables = [pltpu.VMEM((nblk + 8, BLOCK), i32), pltpu.SMEM((nblk + 8, BLOCK), i32)]
        return pl.pallas_call(
            functools.partial(first_kernel, entries, layers, len(arrays)),
            out_shape=jax.ShapeDtypeStruct((2 * nblk, BLOCK, BLOCK), bf16),
            in_specs=[SMEM, VMEM] + [VMEM] * len(arrays),
            out_specs=VMEM,
            scratch_shapes=[pltpu.VMEM((2 * nblk, BLOCK, BLOCK), f32)] + tables,
            cost_estimate=estimate(56 * 2 * BLOCK**3, 10_000_000),
            name="first",
        )(place, packed[1], *arrays)

    def settle(n, group, joined=None):
        arrived = twin_of(group) if joined is None else twin(joined)
        for i, (a, key) in enumerate(group):
            gathered[n].append((arrived, i * a.shape[0], key[:2] + (1,)))
        return arrived

    joined = [None, None]

    def advance(n, t, extra=()):
        cur, last = curs[n], t == layers - 1
        gathered[n].append((cur, 0, (t, 0, 0)))
        waiting[n].append((cur, (t, 0, 0)))
        moves = [across(cur)]
        if last:
            early, pair = waiting[n][:-2], waiting[n][-2:]
            moves.append(settle(n, early, joined[n]))
            moves += ([settle(n, pair)] if n == 0 else [settle(n, [one]) for one in pair])
        else:
            moves.append(up(cur))
            if t == layers - 2:
                moves.append(jnp.concatenate([a for a, _ in waiting[n]], axis=0))
        tied = lax.optimization_barrier((*moves, *extra))
        side = tied[0]
        gathered[n].append((side, 0, (t, 1, 0)))
        if last:
            settle(n, [(side, (t, 1, 0))])
        else:
            waiting[n].append((side, (t, 1, 0)))
            curs[n] = tied[1]
            if t == layers - 2:
                joined[n] = tied[2]
        return list(tied[: len(moves)]), list(tied[len(moves) :])

    ahead, _ = advance(0, 0)
    for t in range(layers):
        if t < layers - 1:
            ahead, _ = advance(0, t + 1)
            advance(1, t, ahead[:1])
        else:
            prods = advance(1, t, [first_product()])[1][0]

    arrays, entries = refs_of(gathered[1])
    tables = [pltpu.VMEM((nblk, BLOCK), i32), pltpu.SMEM((nblk, BLOCK), i32)]
    outs = pl.pallas_call(
        functools.partial(second_kernel, entries, layers, len(arrays)),
        out_shape=[jax.ShapeDtypeStruct((per, BLOCK, BLOCK), f32 if m < half else bf16) for m in masks],
        in_specs=[SMEM, VMEM] + [VMEM] * len(arrays),
        out_specs=[VMEM] * 4,
        scratch_shapes=[pltpu.VMEM((nblk, BLOCK, BLOCK), f32)] + tables,
        cost_estimate=estimate(nblk * 16 * BLOCK**3, 12_000_000),
        name="second",
    )(place, prods, *arrays)

    back = [outs[0]] + [by_mask(m)(o) for m, o in zip(masks[1:], outs[1:], strict=True)]
    return pl.pallas_call(
        join_kernel,
        out_shape=jax.ShapeDtypeStruct((2, 2 * BLOCK, width), f32),
        in_specs=[SMEM, SMEM] + [VMEM] * 4,
        out_specs=VMEM,
        cost_estimate=estimate(0, 8 * BLOCK * width * 4),
        name="join",
    )(place, grad_keep, *back)


def solution(mesh):
    grid = P("row", "col")
    spins = P(None, "row", "col")
    return jax.shard_map(
        functools.partial(body, mesh.shape["row"], mesh.shape["col"]),
        mesh=mesh,
        in_specs=(spins, grid, spins, grid, grid, grid, grid),
        out_specs=spins,
        check_vma=False,
    )
```
